32 devices in a mesh: slab: 16 (over z, x, core), tp: 2 (over y).
Axes of the slice: x: 2, y: 2, z: 4, core: 2. Of those that a mesh axis runs over, the one named last changes fastest.
Arguments:
- tokens: bfloat16 [16384, 512], P('slab', 'tp'), may hold values from -8 to 8
- stem_taps: float32 [3, 512], P(None, 'tp'), may hold values from 0.1 to 1.9
- query_weight: bfloat16 [512, 512], P(None, 'tp'), may hold values from -0.25 to 0.25
- key_weight: bfloat16 [512, 512], P(None, 'tp'), may hold values from -0.25 to 0.25
- value_weight: bfloat16 [512, 512], P(None, 'tp'), may hold values from -0.25 to 0.25
- out_weight: bfloat16 [512, 512], P('tp'), may hold values from -0.25 to 0.25
- key_blocks: int32 [128, 4], P('slab'), may hold values from 0 to 127, as said below
- counts: int32 [128], P('slab'), may hold values from 3 to 4, as said below
- cotangent: bfloat16 [16384, 512], P('slab', 'tp'), may hold values from -6 to 6
Outputs:
- layer_out: bfloat16 [16384, 512], P('slab', 'tp')
- grad_tokens: float32 [16384, 512], P('slab', 'tp')
- grad_taps: float32 [3, 512], P(None, 'tp')
- grad_query_weight: float32 [512, 512], P(None, 'tp')
- grad_key_weight: float32 [512, 512], P(None, 'tp')
- grad_value_weight: float32 [512, 512], P(None, 'tp')
- grad_out_weight: float32 [512, 512], P('tp')
The draws below stay inside these ranges and needn't reach their ends.
Inputs may be any that keep to these rules, and one draw needn't show every extreme that they name: `key_blocks`: query block i lies in plane p = i // 4. Its slots 0, 1, 2 name the block at the same position in planes p, p - 1 and p + 1 (planes modulo 32); every live slot names a different block of these three planes; slots from counts[i] on name block i itself. `counts`: some query block has all 4 slots live; loads differ from plane to plane.
All inputs are finite; a program needn't handle non-finite values.
Results may differ from the reference program's by a relative error of at most 0.009.
The reference program's roundings to bfloat16 on the way count: a program that leaves them out, or rounds other values in their place, can miss the bound.
Values may be sent and summed in bfloat16 or wider, within the bound.
A program may use at most 128 MiB of HBM per device.

```python
import jax
import jax.numpy as jnp
from jax import lax

D = 512
HEADS = 8
HD = 64
BLK = 128
PLANE_TOK = 512
MAXK = 4
TOKENS = 16384
NPLANES = 32


def draw_tokens(key, part):
    key_normal = jax.random.fold_in(key, 0)
    values = jax.random.normal(key_normal, (TOKENS, D), jnp.float32)
    return jnp.clip(values, -8.0, 8.0).astype(jnp.bfloat16)


def shared_pattern(key):
    pattern_key = jax.random.fold_in(key, 11)
    key_rank, key_cap, key_count = jax.random.split(pattern_key, 3)
    per_plane = PLANE_TOK // BLK
    block_total = NPLANES * per_plane
    query_ids = jnp.arange(block_total, dtype=jnp.int32)
    plane_ids = query_ids // per_plane
    block_pos = query_ids % per_plane

    def rank_row(row_key):
        return jax.random.permutation(row_key, 3 * per_plane)
    rank_rows = jax.vmap(rank_row)(jax.random.split(key_rank, block_total)).astype(jnp.int32)
    candidate = jnp.arange(3 * per_plane, dtype=jnp.int32)[None, :]
    priority = jnp.where(candidate == per_plane + block_pos[:, None], -3, jnp.where(candidate == block_pos[:, None], -2, jnp.where(candidate == 2 * per_plane + block_pos[:, None], -1, rank_rows)))
    slot_order = jnp.argsort(priority, axis=1)[:, :MAXK].astype(jnp.int32)
    key_plane = jnp.remainder(plane_ids[:, None] + slot_order // per_plane - 1, NPLANES)
    chosen = key_plane * per_plane + slot_order % per_plane
    plane_caps = jax.random.randint(key_cap, (NPLANES,), 3, MAXK + 1)
    live_counts = 3 + jax.random.randint(key_count, (block_total,), 0, plane_caps[plane_ids] - 2)
    live_counts = live_counts.at[0].set(MAXK)
    slot_ids = jnp.arange(MAXK, dtype=jnp.int32)[None, :]
    chosen = jnp.where(slot_ids < live_counts[:, None], chosen, query_ids[:, None])
    return (chosen.astype(jnp.int32), live_counts.astype(jnp.int32))


def draw_key_blocks(key, part):
    return shared_pattern(key)[0]


def draw_counts(key, part):
    return shared_pattern(key)[1]


def level_of(key, extent, shards, smallest, high):
    level, own = 1.0, jax.random.fold_in(key, 6)
    for axis_at, blocks in shards:
        heights = jnp.exp(jax.random.uniform(jax.random.fold_in(own, axis_at), (blocks,), jnp.float32, smallest / len(shards), high / len(shards)))
        level = level * jnp.repeat(heights, extent[axis_at] // blocks).reshape([-1 if axis == axis_at else 1 for axis in range(len(extent))])
    return level


def gaussian(stream_key, dims, spread, most, cuts=(), kind=jnp.bfloat16):
    result = jax.random.normal(stream_key, dims, jnp.float32) * spread
    if len(cuts) > 0:
        result = level_of(stream_key, dims, cuts, -0.22, 0.18) * result
    return jnp.clip(result, min=-most, max=most).astype(kind)


def setup_inputs(seed: int = 0) -> dict:
    key_list = jax.random.split(jax.random.key(seed), 10)
    return {
        "tokens": draw_tokens(jax.random.fold_in(key_list[9], 71), 0),
        "stem_taps": jnp.clip(1.0 + 0.18 * jax.random.normal(key_list[1], (3, D), jnp.float32), 0.1, 1.9),
        "query_weight": gaussian(key_list[2], (D, D), D ** -0.5, 0.25, ((1, 2),)),
        "key_weight": gaussian(key_list[3], (D, D), D ** -0.5, 0.25, ((1, 2),)),
        "value_weight": gaussian(key_list[4], (D, D), D ** -0.5, 0.25, ((1, 2),)),
        "out_weight": gaussian(key_list[5], (D, D), D ** -0.5, 0.25, ((0, 2),)),
        "key_blocks": draw_key_blocks(jax.random.fold_in(key_list[9], 71), 0),
        "counts": draw_counts(jax.random.fold_in(key_list[9], 71), 0),
        "cotangent": gaussian(key_list[8], (TOKENS, D), 1.0, 6.0, ((0, 16), (1, 2))),
    }


NEG = -1e30


def softmax_scores(query_block, key_block, live_counts):
    scores = jnp.einsum("gqhd,gkhd->ghqk", query_block, key_block) * (HD ** -0.5)
    slot_ids = jnp.arange(key_block.shape[1]) // BLK
    live_mask = slot_ids[None, :] < live_counts[:, None]
    scores = jnp.where(live_mask[:, None, None, :], scores, NEG)
    row_max = jnp.max(scores, axis=-1, keepdims=True)
    exp_scores = jnp.exp(scores - row_max)
    return exp_scores / jnp.sum(exp_scores, axis=-1, keepdims=True)


def reference(tokens, stem_taps, query_weight, key_weight, value_weight, out_weight, key_blocks, counts, cotangent):
    inputs_f = tokens.astype(jnp.float32)
    before_rows = jnp.roll(inputs_f, PLANE_TOK, axis=0)
    after_rows = jnp.roll(inputs_f, -PLANE_TOK, axis=0)
    stem_rows = (stem_taps[0] * before_rows + stem_taps[1] * inputs_f + stem_taps[2] * after_rows).astype(jnp.bfloat16)
    query_rows = jnp.dot(stem_rows, query_weight, preferred_element_type=jnp.float32).astype(jnp.bfloat16)
    key_rows = jnp.dot(stem_rows, key_weight, preferred_element_type=jnp.float32).astype(jnp.bfloat16)
    value_rows = jnp.dot(stem_rows, value_weight, preferred_element_type=jnp.float32).astype(jnp.bfloat16)
    block_total = TOKENS // BLK
    groups = block_total // 4
    key_all = key_rows.reshape(block_total, BLK, HEADS, HD)
    value_all = value_rows.reshape(block_total, BLK, HEADS, HD)
    query_groups = query_rows.reshape(groups, 4, BLK, HEADS, HD)
    index_groups = key_blocks.reshape(groups, 4, MAXK).astype(jnp.int32)
    count_groups = counts.reshape(groups, 4)

    def fetch(table, block_ids):
        picked = jnp.take(table, block_ids.reshape(-1), axis=0)
        return picked.reshape(4, MAXK * BLK, HEADS, HD).astype(jnp.float32)

    def forward_group(inputs):
        query_block, block_ids, live_counts = inputs
        key_block = fetch(key_all, block_ids)
        value_block = fetch(value_all, block_ids)
        attn_probs = softmax_scores(query_block.astype(jnp.float32), key_block, live_counts)
        probs_low = lax.optimization_barrier(attn_probs.astype(jnp.bfloat16)).astype(jnp.float32)
        return jnp.einsum("ghqk,gkhd->gqhd", probs_low, value_block).astype(jnp.bfloat16)

    attn = lax.map(forward_group, (query_groups, index_groups, count_groups)).reshape(TOKENS, D)
    mixed_rows = jnp.dot(attn, out_weight, preferred_element_type=jnp.float32)
    layer_out = (stem_rows.astype(jnp.float32) + mixed_rows).astype(jnp.bfloat16)

    grad_attn = jnp.dot(cotangent, out_weight.T, preferred_element_type=jnp.float32).astype(jnp.bfloat16)
    grad_out_weight = jnp.dot(attn.T, cotangent, preferred_element_type=jnp.float32)
    grad_groups = grad_attn.reshape(groups, 4, BLK, HEADS, HD)

    def backward_group(grad_pairs, inputs):
        query_block, block_ids, live_counts, grad_block = inputs
        query_f = query_block.astype(jnp.float32)
        grad_f = grad_block.astype(jnp.float32)
        key_block = fetch(key_all, block_ids)
        value_block = fetch(value_all, block_ids)
        attn_probs = softmax_scores(query_f, key_block, live_counts)
        probs_low = lax.optimization_barrier(attn_probs.astype(jnp.bfloat16)).astype(jnp.float32)
        grad_probs = jnp.einsum("gqhd,gkhd->ghqk", grad_f, value_block)
        row_inner = jnp.sum(attn_probs * grad_probs, axis=-1, keepdims=True)
        grad_scores = attn_probs * (grad_probs - row_inner) * (HD ** -0.5)
        grad_scores = lax.optimization_barrier(grad_scores.astype(jnp.bfloat16)).astype(jnp.float32)
        grad_query = jnp.einsum("ghqk,gkhd->gqhd", grad_scores, key_block).astype(jnp.bfloat16)
        grad_key = jnp.einsum("ghqk,gqhd->gkhd", grad_scores, query_f)
        grad_value = jnp.einsum("ghqk,gqhd->gkhd", probs_low, grad_f)
        slot_rows = jnp.stack([grad_key, grad_value]).reshape(2, 4 * MAXK, BLK, D)
        grad_pairs = grad_pairs.at[:, block_ids.reshape(-1)].add(slot_rows)
        return grad_pairs, grad_query

    start_pairs = jnp.zeros((2, block_total, BLK, D), jnp.float32)
    grad_pairs, grad_query = lax.scan(backward_group, start_pairs, (query_groups, index_groups, count_groups, grad_groups))
    grad_query = grad_query.reshape(TOKENS, D)
    grad_key = grad_pairs[0].reshape(TOKENS, D).astype(jnp.bfloat16)
    grad_value = grad_pairs[1].reshape(TOKENS, D).astype(jnp.bfloat16)
    grad_stem = cotangent.astype(jnp.float32) + (jnp.dot(grad_query, query_weight.T, preferred_element_type=jnp.float32) + jnp.dot(grad_key, key_weight.T, preferred_element_type=jnp.float32) + jnp.dot(grad_value, value_weight.T, preferred_element_type=jnp.float32))
    grad_tokens = stem_taps[0] * jnp.roll(grad_stem, -PLANE_TOK, axis=0) + stem_taps[1] * grad_stem + stem_taps[2] * jnp.roll(grad_stem, PLANE_TOK, axis=0)
    grad_taps = jnp.stack([jnp.sum(grad_stem * before_rows, axis=0), jnp.sum(grad_stem * inputs_f, axis=0), jnp.sum(grad_stem * after_rows, axis=0)])
    grad_query_weight = jnp.dot(stem_rows.T, grad_query, preferred_element_type=jnp.float32)
    grad_key_weight = jnp.dot(stem_rows.T, grad_key, preferred_element_type=jnp.float32)
    grad_value_weight = jnp.dot(stem_rows.T, grad_value, preferred_element_type=jnp.float32)
    return (layer_out, grad_tokens, grad_taps, grad_query_weight, grad_key_weight, grad_value_weight, grad_out_weight)
```

```python
import functools

import jax
import jax.numpy as jnp
from jax import lax
from jax.experimental import pallas as pl
from jax.experimental.pallas import tpu as pltpu
from jax.sharding import PartitionSpec as P

HD = 64
BLK = 128
PLANE_TOK = 512
MAXK = 4
NEG = -1e30
F32 = jnp.float32
BF16 = jnp.bfloat16
MESH = pl.DeviceIdType.MESH
VMEM = pl.BlockSpec(memory_space=pltpu.VMEM)
SMEM = pl.BlockSpec(memory_space=pltpu.SMEM)
MIB = 1024 * 1024
CHUNK = 256


def mm(a, b):
    return jnp.dot(a, b, preferred_element_type=F32)


def mm_nt(a, b):
    return lax.dot_general(a, b, (((1,), (1,)), ((), ())), preferred_element_type=F32)


def mm_tn(a, b):
    return lax.dot_general(a, b, (((0,), (0,)), ((), ())), preferred_element_type=F32)


def part(index, width):
    return pl.ds(pl.multiple_of(index * width, width), width)


def copy_to(src, dst, send, recv, where):
    return pltpu.make_async_remote_copy(
        src_ref=src,
        dst_ref=dst,
        send_sem=send,
        recv_sem=recv,
        device_id=where,
        device_id_type=MESH,
    )


def layer_kernel(
    slabs,
    blocks_ref,
    counts_ref,
    tok_ref,
    cot_ref,
    taps_ref,
    wq_ref,
    wk_ref,
    wv_ref,
    ow_ref,
    layer_ref,
    grad_ref,
    final,
    taps_out_ref,
    halo,
    so,
    st,
    ct,
    q,
    kv,
    grad,
    attn,
    acc,
    spare,
    gq_all,
    low,
    from_halo,
    mix,
    mix_out,
    mix_in,
    own,
    other,
    part_out,
    part_in,
    edge,
    edge_in,
    wsum,
    outgoing,
    incoming,
    taps_in,
    taps_sum,
    t_send,
    t_recv,
    s_send,
    s_recv,
    c_send,
    c_recv,
    so_send,
    so_recv,
    st_send,
    st_recv,
    h_send,
    h_recv,
    m_send,
    m_recv,
    p_send,
    p_recv,
    e_send,
    e_recv,
    w_send,
    w_recv,
    g_send,
    g_recv,
):
    me = lax.axis_index("slab")
    tp = lax.axis_index("tp")
    core = lax.rem(me, 2)
    bits = tuple(range(slabs.bit_length() - 1))
    stages = len(bits)
    tokens, width = tok_ref.shape
    cols, depth = ow_ref.shape
    heads = cols // HD
    planes = tokens // PLANE_TOK
    total = planes * slabs
    per_plane = PLANE_TOK // BLK
    pieces = PLANE_TOK // CHUNK
    halves = cols // 128
    last = planes - 1
    span = wsum.shape[0] // 2
    mine, theirs = part(tp, width), part(1 - tp, width)
    mate = {"tp": 1 - tp}
    slow = {"slab": lax.rem(me + slabs + 2 * core - 1, slabs)}
    fast = {"slab": me + 1 - 2 * core}
    sides = (slow, fast)
    sent = []

    def bit_of(b):
        return lax.rem(lax.div(me, 1 << b), 2)

    def partner(b):
        return {"slab": me + (1 - 2 * bit_of(b)) * (1 << b)}

    def plane_of(k):
        return core * last + (1 - 2 * core) * k

    def nat(k, c, size=CHUNK):
        return pl.ds(pl.multiple_of(plane_of(k) * PLANE_TOK + c * size, size), size)

    def loc(k, c, size=CHUNK):
        return pl.ds(k * PLANE_TOK + c * size, size)

    barrier = pltpu.get_barrier_semaphore()
    for where in [slow, mate] + [partner(b) for b in bits]:
        pl.semaphore_signal(barrier, inc=1, device_id=where, device_id_type=MESH)
    pl.semaphore_wait(barrier, stages + 2)

    def launch(copy):
        copy.start()
        sent.append(copy)
        return copy

    halos = {}
    for c in range(pieces):
        for side, k in ((0, 0), (1, last)):
            halos[side, c] = launch(
                copy_to(
                    tok_ref.at[nat(k, c)], halo.at[side, loc(0, c)],
                    t_send.at[side, c], t_recv.at[side, c], sides[side],
                )
            )
    cots = {
        (k, c): copy_to(
            cot_ref.at[nat(k, c)], ct.at[nat(k, c)],
            c_send.at[k * pieces + c], c_recv.at[k * pieces + c], mate,
        )
        for k in range(planes)
        for c in range(pieces)
    }
    waiting = list(cots)
    launch(cots[waiting.pop(0)])

    tap_low = taps_ref[pl.ds(2 * core, 1), :]
    tap_mid = taps_ref[1:2, :]
    tap_high = taps_ref[pl.ds(2 - 2 * core, 1), :]

    def tokens_at(k, c):
        if k < 0:
            return halo[0, loc(0, c), :].astype(F32)
        if k > last:
            return halo[1, loc(0, c), :].astype(F32)
        return tok_ref[nat(k, c), :].astype(F32)

    def edges_of(k):
        return [(0, 0)] * (k == 0) + [(1, planes + 1)] * (k == last)

    order = [(k, c) for k in reversed(range(planes)) for c in range(pieces)]
    stems, so_halo, st_halo = {}, {}, {}
    for k, c in order:
        for side, _ in edges_of(k):
            halos[side, c].wait_recv()
        rows = loc(k + 1, c)
        so[rows, :] = (
            tap_low * tokens_at(k - 1, c) + tap_mid * tokens_at(k, c) + tap_high * tokens_at(k + 1, c)
        ).astype(BF16)
        stems[k, c] = launch(
            copy_to(
                so.at[rows], st.at[rows], s_send.at[k * pieces + c], s_recv.at[k * pieces + c], mate
            )
        )
        for side, e in edges_of(k):
            so_halo[side, c] = launch(
                copy_to(
                    so.at[rows], so.at[loc(e, c)],
                    so_send.at[side, c], so_recv.at[side, c], sides[side],
                )
            )

    def project(w_ref, rows):
        return (mm(so[rows, :], w_ref[mine, :]) + mm(st[rows, :], w_ref[theirs, :])).astype(BF16)

    def keys_values(rows):
        for half, w_ref in enumerate((wk_ref, wv_ref)):
            value = project(w_ref, rows)
            for n in range(CHUNK // BLK):
                kv[rows.start // BLK + n, :, half * cols : (half + 1) * cols] = value[
                    n * BLK : (n + 1) * BLK
                ]

    for n, (k, c) in enumerate(order):
        rows = loc(k + 1, c)
        stems[k, c].wait_recv()
        for side, e in edges_of(k):
            st_halo[side, c] = launch(
                copy_to(
                    st.at[rows], st.at[loc(e, c)],
                    st_send.at[side, c], st_recv.at[side, c], sides[side],
                )
            )
        if n == len(order) - 2:
            launch(cots[waiting.pop(0)])
        if n == len(order) - 1:
            for name in waiting:
                launch(cots[name])
        keys_values(rows)
        q[nat(k, c), :] = project(wq_ref, rows)

    def output_gradient(k):
        for c in range(pieces):
            rows = nat(k, c)
            cots[k, c].wait_recv()
            grad[rows, :] = (
                mm_nt(cot_ref[rows, :], ow_ref[:, mine]) + mm_nt(ct[rows, :], ow_ref[:, theirs])
            ).astype(BF16)

    def halo_keys(side, e):
        for c in range(pieces):
            so_halo[side, c].wait_recv()
            st_halo[side, c].wait_recv()
            keys_values(loc(e, c))

    halo_keys(1, planes + 1)
    output_gradient(0)
    halo_keys(0, 0)

    lane = lax.broadcasted_iota(jnp.int32, (1, cols), 1) // HD
    masks = [(lane == h).astype(F32).astype(BF16) for h in range(heads)]

    def stack(block):
        return jnp.concatenate([block * mask for mask in masks], axis=0)

    def pick(value):
        heads_t = [
            value[h * HD : (h + 1) * HD, h * BLK : (h + 1) * BLK] for h in range(heads)
        ]
        return jnp.concatenate(heads_t, axis=0).T

    def free_slot(k, j):
        block = blocks_ref[MAXK - 1, plane_of(k) * per_plane + j]
        plane = lax.rem(
            lax.div(block, per_plane) - me * planes - plane_of(k) + 1 + total, total
        )
        plane = k + core * 2 + (1 - 2 * core) * jnp.minimum(plane, 2)
        return plane * per_plane + lax.rem(block, per_plane)

    def attention(k):
        @pl.loop(0, per_plane)
        def _(j):
            rows = nat(k, j, BLK)
            places = [
                pl.ds(pl.multiple_of(e * PLANE_TOK + j * BLK, BLK), BLK) for e in range(k, k + 3)
            ]
            where = [e * per_plane + j for e in range(k, k + 3)] + [free_slot(k, j)]
            pairs = [kv[at] for at in where]
            keys = jnp.concatenate([pair[:, :cols] for pair in pairs], axis=0)
            values = jnp.concatenate([pair[:, cols:] for pair in pairs], axis=0)
            queries = stack(q[rows, :] * jnp.asarray(HD**-0.5, BF16))
            grads = stack(grad[rows, :])
            scores = mm_nt(keys, queries)
            left_out = MAXK - counts_ref[plane_of(k) * per_plane + j]
            fixed = (MAXK - 1) * BLK
            scores = jnp.concatenate(
                [scores[:fixed], scores[fixed:] + left_out.astype(F32) * NEG], axis=0
            )
            exps = jnp.exp(scores - jnp.max(scores, axis=0, keepdims=True))
            probs = exps * (1.0 / jnp.sum(exps, axis=0, keepdims=True))
            round_probs = probs.astype(BF16)
            attn[rows, :] = pick(mm_tn(values, round_probs)).astype(BF16)
            gprobs = mm_nt(values, grads)
            inner = jnp.sum(probs * gprobs, axis=0, keepdims=True)
            gscores = (probs * (gprobs - inner)).astype(BF16)
            at = pl.ds(pl.multiple_of(k * PLANE_TOK + j * BLK, BLK), BLK)
            gq_all[at, :] = (pick(mm_tn(keys, gscores)) * (HD**-0.5)).astype(BF16)
            gkeys = mm(gscores, queries)
            gvalues = mm(round_probs, grads)
            for n, place in enumerate(places):
                for half, g in enumerate((gkeys, gvalues)):
                    columns = slice(half * cols, (half + 1) * cols)
                    block = g[n * BLK : (n + 1) * BLK]
                    if k == 0 or n == 2:
                        acc[place, columns] = block
                    else:
                        acc[place, columns] += block
            spare[k * per_plane + j, :, 0:cols] = gkeys[fixed:]
            spare[k * per_plane + j, :, cols : 2 * cols] = gvalues[fixed:]

    def collect(e):
        @pl.loop(0, per_plane)
        def _(t):
            at = pl.ds(pl.multiple_of(e * PLANE_TOK + t * BLK, BLK), BLK)
            value = acc[at, :]
            for k in range(max(e - 2, 0), min(e, last) + 1):
                for step in range(1, per_plane):
                    j = lax.rem(t + step, per_plane)
                    off = free_slot(k, j) - (e * per_plane + t)
                    hit = (1 - jnp.minimum(off * off, 1)).astype(F32)
                    value = value + hit * spare[k * per_plane + j]
            if 1 <= e <= planes:
                acc[at, :] = value
            low[at, :] = value.astype(BF16)

    returns = {}

    def give_back(side, e):
        rows = loc(e, 0, PLANE_TOK)
        returns[side] = launch(
            copy_to(
                low.at[rows], from_halo.at[side], h_send.at[side], h_recv.at[side], sides[side]
            )
        )

    mixes = {}

    def mix_heads(k):
        rows = nat(k, 0, PLANE_TOK)
        mix_out[rows, :] = mm(attn[rows, :], ow_ref[:, theirs]).astype(BF16)
        mixes[k] = launch(
            copy_to(mix_out.at[rows], mix_in.at[rows], m_send.at[k], m_recv.at[k], mate)
        )
        mix[rows, :] = mm(attn[rows, :], ow_ref[:, mine])

    for k in range(planes):
        if k > 0:
            output_gradient(k)
        attention(k)
        if k == 0:
            collect(0)
            give_back(0, 0)
        if k == last:
            collect(planes + 1)
            give_back(1, planes + 1)
        mix_heads(k)

    orders = (bits[:1] + bits[2:] + bits[1:2], bits)
    lows = [jnp.int32(0), jnp.int32(span)]
    trail = [[], []]
    step_of = [0, 0]
    flight = [None, None]

    def rows_at(at, size):
        return pl.ds(pl.multiple_of(at, 16), size)

    def advance(t):
        k = step_of[t]
        if k > 2 * stages:
            return
        if flight[t] is not None:
            flight[t].wait_recv()
            if k <= stages:
                size = span >> k
                at = rows_at(lows[t], size)
                offset = span - 2 * size
                wsum[at, :] = wsum[at, :] + incoming[t, pl.ds(offset, size), :].astype(F32)
        if k == stages:
            at = rows_at(lows[t], span >> stages)
            final[at, :] = wsum[at, :].astype(BF16)
        if k < stages:
            size = span >> (k + 1)
            b = orders[t][k]
            bit = bit_of(b)
            keep = lows[t] + bit * size
            give = lows[t] + (1 - bit) * size
            slots = pl.ds(span - 2 * size, size)
            outgoing[t, slots, :] = wsum[rows_at(give, size), :].astype(BF16)
            flight[t] = launch(
                copy_to(
                    outgoing.at[t, slots], incoming.at[t, slots],
                    w_send.at[t, k], w_recv.at[t, k], partner(b),
                )
            )
            lows[t] = keep
            trail[t].append(keep)
        elif k < 2 * stages:
            j = 2 * stages - 1 - k
            at = rows_at(trail[t][j], span >> (j + 1))
            flight[t] = launch(
                copy_to(
                    final.at[at], final.at[at],
                    w_send.at[t, k], w_recv.at[t, k], partner(orders[t][j]),
                )
            )
        step_of[t] = k + 1

    def weight_gradient(base, rows, g):
        for index, s_ref in ((tp, so), (1 - tp, st)):
            product = mm_tn(s_ref[rows, :], g)
            for half in range(halves):
                at = pl.multiple_of(base + half * depth + index * width, 128)
                wsum[pl.ds(at, width), :] = product[:, half * 128 : (half + 1) * 128]

    block = depth * halves
    inside = slice(PLANE_TOK, PLANE_TOK + tokens)
    weight_gradient(0, inside, gq_all[...])
    for index, c_ref in ((tp, cot_ref), (1 - tp, ct)):
        product = mm_tn(attn[...], c_ref[...])
        for half in range(width // 128):
            wsum[pl.ds(pl.multiple_of(block + (index * (width // 128) + half) * cols, 128), cols), :] = (
                product[:, half * 128 : (half + 1) * 128]
            )
    advance(0)
    for e in range(1, planes + 1):
        collect(e)
    everything = slice(0, low.shape[0])
    weight_gradient(2 * block, everything, low[:, :cols])
    weight_gradient(3 * block, everything, low[:, cols:])
    advance(1)
    advance(0)
    for k in range(planes):
        for c in range(pieces):
            rows = loc(k, c)
            gq = gq_all[rows, :]
            own[rows, :] = mm_nt(gq, wq_ref[mine, :])
            other[rows, :] = mm_nt(gq, wq_ref[theirs, :])
    advance(1)
    parts = {}
    for k in range(planes):
        for side, _ in edges_of(k):
            returns[side].wait_recv()
        for c in range(pieces):
            rows = loc(k, c)
            value = acc[loc(k + 1, c), :]
            for side, _ in edges_of(k):
                value = value + from_halo[side, loc(0, c), :].astype(F32)
            value = value.astype(BF16)
            gk, gv = value[:, :cols], value[:, cols:]
            part_out[rows, :] = (
                other[rows, :] + mm_nt(gk, wk_ref[theirs, :]) + mm_nt(gv, wv_ref[theirs, :])
            ).astype(BF16)
            parts[k, c] = launch(
                copy_to(
                    part_out.at[rows], part_in.at[rows],
                    p_send.at[k * pieces + c], p_recv.at[k * pieces + c], mate,
                )
            )
            own[rows, :] += mm_nt(gk, wk_ref[mine, :]) + mm_nt(gv, wv_ref[mine, :])
        advance(0)
        advance(1)
    for k in range(planes):
        rows = nat(k, 0, PLANE_TOK)
        mixes[k].wait_recv()
        layer_ref[rows, :] = (
            so[loc(k + 1, 0, PLANE_TOK), :].astype(F32) + (mix[rows, :] + mix_in[rows, :].astype(F32))
        ).astype(BF16)
    advance(0)
    advance(1)
    edges = {}
    for k in range(planes):
        for c in range(pieces):
            rows = loc(k, c)
            parts[k, c].wait_recv()
            stem_grad = cot_ref[nat(k, c), :].astype(F32) + (
                own[rows, :] + part_in[rows, :].astype(F32)
            )
            own[rows, :] = stem_grad
            for side, _ in edges_of(k):
                at = loc(side, c)
                edge[at, :] = stem_grad.astype(BF16)
                edges[side, c] = launch(
                    copy_to(
                        edge.at[at], edge_in.at[at],
                        e_send.at[side, c], e_recv.at[side, c], sides[side],
                    )
                )
        advance(0)
        advance(1)
    sums = [jnp.zeros((1, width), F32) for _ in range(3)]
    for k in range(planes):
        for c in range(pieces):
            g = own[loc(k, c), :]
            for n in range(3):
                sums[n] = sums[n] + jnp.sum(g * tokens_at(k - 1 + n, c), axis=0, keepdims=True)
    swap = core == 1
    sums = [jnp.where(swap, sums[2], sums[0]), sums[1], jnp.where(swap, sums[0], sums[2])]
    taps_sum[0] = jnp.concatenate(sums + [jnp.zeros((5, width), F32)], axis=0)

    def send_taps(k):
        return launch(
            copy_to(taps_sum.at[k], taps_in.at[k], g_send.at[k], g_recv.at[k], partner(bits[k]))
        )

    def take_taps(k, copy):
        copy.wait_recv()
        taps_sum[k + 1] = taps_sum[k] + taps_in[k]

    def gradient_at(k, c):
        if k < 0:
            return edge_in[loc(0, c), :].astype(F32)
        if k > last:
            return edge_in[loc(1, c), :].astype(F32)
        return own[loc(k, c), :]

    def finish_tokens():
        for copy in edges.values():
            copy.wait_recv()
        for k in range(planes):
            for c in range(pieces):
                grad_ref[nat(k, c), :] = (
                    tap_low * gradient_at(k + 1, c) + tap_mid * gradient_at(k, c)
                    + tap_high * gradient_at(k - 1, c)
                )

    for k in range(stages):
        copy = send_taps(k)
        advance(1)
        advance(0)
        if k == 1:
            finish_tokens()
        take_taps(k, copy)
    if stages < 2:
        finish_tokens()
    for _ in range(2 * stages):
        advance(0)
        advance(1)
    taps_out_ref[...] = taps_sum[stages]
    for copy in sent:
        copy.wait_send()


def unpack_kernel(final_ref, taps_in_ref, gqw_ref, gkw_ref, gvw_ref, go_ref, taps_ref):
    at = 0
    for out in (gqw_ref, go_ref, gkw_ref, gvw_ref):
        rows = out.shape[0]
        for half in range(out.shape[1] // 128):
            out[:, half * 128 : (half + 1) * 128] = final_ref[at : at + rows, :].astype(F32)
            at += rows
    taps_ref[...] = taps_in_ref[0:3, :]


def body(
    slabs,
    tokens,
    stem_taps,
    query_weight,
    key_weight,
    value_weight,
    out_weight,
    key_blocks,
    counts,
    cotangent,
):
    count, width = tokens.shape
    depth, cols = query_weight.shape
    plane = PLANE_TOK
    planes = count // plane
    sds = jax.ShapeDtypeStruct
    params = pltpu.CompilerParams(vmem_limit_bytes=20 * MIB)
    stages = slabs.bit_length() - 1
    chunks = count // CHUNK
    pieces = plane // CHUNK
    blocks = count // BLK
    wide = count + 2 * plane
    dma = pltpu.SemaphoreType.DMA
    rows = 4 * depth * cols // 128
    semaphores = [
        (2, pieces),
        (chunks,),
        (chunks,),
        (2, pieces),
        (2, pieces),
        (2,),
        (planes,),
        (chunks,),
        (2, pieces),
        (2, 2 * stages),
        (stages,),
    ]
    layer_out, grad_tokens, final, taps = pl.pallas_call(
        functools.partial(layer_kernel, slabs),
        out_shape=[
            sds((count, width), BF16),
            sds((count, width), F32),
            sds((rows, 128), BF16),
            sds((8, width), F32),
        ],
        in_specs=[SMEM] * 2 + [VMEM] * 7,
        out_specs=[VMEM] * 4,
        scratch_shapes=[
            pltpu.VMEM((2, plane, width), BF16),
            pltpu.VMEM((wide, width), BF16),
            pltpu.VMEM((wide, width), BF16),
            pltpu.VMEM((count, width), BF16),
            pltpu.VMEM((count, cols), BF16),
            pltpu.VMEM((wide // BLK, BLK, 2 * cols), BF16),
            pltpu.VMEM((count, cols), BF16),
            pltpu.VMEM((count, cols), BF16),
            pltpu.VMEM((wide, 2 * cols), F32),
            pltpu.VMEM((blocks, BLK, 2 * cols), F32),
            pltpu.VMEM((count, cols), BF16),
            pltpu.VMEM((wide, 2 * cols), BF16),
            pltpu.VMEM((2, plane, 2 * cols), BF16),
            pltpu.VMEM((count, width), F32),
            pltpu.VMEM((count, width), BF16),
            pltpu.VMEM((count, width), BF16),
            pltpu.VMEM((count, width), F32),
            pltpu.VMEM((count, width), F32),
            pltpu.VMEM((count, width), BF16),
            pltpu.VMEM((count, width), BF16),
            pltpu.VMEM((2 * plane, width), BF16),
            pltpu.VMEM((2 * plane, width), BF16),
            pltpu.VMEM((rows, 128), F32),
            pltpu.VMEM((2, rows // 2, 128), BF16),
            pltpu.VMEM((2, rows // 2, 128), BF16),
            pltpu.VMEM((stages, 8, width), F32),
            pltpu.VMEM((stages + 1, 8, width), F32),
        ]
        + [dma(shape) for shape in semaphores for _ in range(2)],
        compiler_params=pltpu.CompilerParams(
            collective_id=0, has_side_effects=True, vmem_limit_bytes=44 * MIB
        ),
    )(
        key_blocks.T,
        counts,
        tokens,
        cotangent,
        stem_taps,
        query_weight,
        key_weight,
        value_weight,
        out_weight,
    )
    gqw, gkw, gvw, go, grad_taps = pl.pallas_call(
        unpack_kernel,
        out_shape=[sds((depth, cols), F32)] * 3
        + [sds((cols, depth), F32), sds(stem_taps.shape, F32)],
        in_specs=[VMEM] * 2,
        out_specs=[VMEM] * 5,
        compiler_params=params,
    )(final, taps)
    return (layer_out, grad_tokens, grad_taps, gqw, gkw, gvw, go)


def solution(mesh):
    in_specs = (
        P("slab", "tp"),
        P(None, "tp"),
        P(None, "tp"),
        P(None, "tp"),
        P(None, "tp"),
        P("tp", None),
        P("slab", None),
        P("slab"),
        P("slab", "tp"),
    )
    out_specs = (
        P("slab", "tp"),
        P("slab", "tp"),
        P(None, "tp"),
        P(None, "tp"),
        P(None, "tp"),
        P(None, "tp"),
        P("tp", None),
    )
    return jax.shard_map(
        functools.partial(body, mesh.shape["slab"]),
        mesh=mesh,
        in_specs=in_specs,
        out_specs=out_specs,
        check_vma=False,
    )
```

```python
import functools

import jax
import jax.numpy as jnp
from jax import lax
from jax.experimental import pallas as pl
from jax.experimental.pallas import tpu as pltpu
from jax.sharding import PartitionSpec as P

HD = 64
BLK = 128
PLANE_TOK = 512
MAXK = 4
NEG = -1e30
F32 = jnp.float32
BF16 = jnp.bfloat16
MESH = pl.DeviceIdType.MESH
VMEM = pl.BlockSpec(memory_space=pltpu.VMEM)
HBM = pl.BlockSpec(memory_space=pltpu.HBM)
MIB = 1024 * 1024
CHUNK = 256


def mm(a, b):
    return jnp.dot(a, b, preferred_element_type=F32)


def mm_nt(a, b):
    return lax.dot_general(a, b, (((1,), (1,)), ((), ())), preferred_element_type=F32)


def mm_tn(a, b):
    return lax.dot_general(a, b, (((0,), (0,)), ((), ())), preferred_element_type=F32)


def part(index, width):
    return pl.ds(pl.multiple_of(index * width, width), width)


def copy_to(src, dst, send, recv, where):
    return pltpu.make_async_remote_copy(
        src_ref=src,
        dst_ref=dst,
        send_sem=send,
        recv_sem=recv,
        device_id=where,
        device_id_type=MESH,
    )


def layer_kernel(
    slabs,
    blocks_in,
    counts_in,
    tok_in,
    cot_in,
    taps_in_ref,
    wq_in,
    wk_in,
    wv_in,
    ow_in,
    layer_ref,
    grad_ref,
    final,
    taps_out_ref,
    blocks_ref,
    counts_ref,
    tok_ref,
    cot_ref,
    taps_ref,
    wq_ref,
    wk_ref,
    wv_ref,
    ow_ref,
    load_sem,
    halo,
    so,
    st,
    ct,
    q,
    kv,
    grad,
    attn,
    acc,
    spare,
    gq_all,
    low,
    from_halo,
    mix,
    mix_out,
    mix_in,
    own,
    other,
    part_out,
    part_in,
    edge,
    edge_in,
    wsum,
    outgoing,
    incoming,
    taps_in,
    taps_sum,
    t_send,
    t_recv,
    s_send,
    s_recv,
    c_send,
    c_recv,
    so_send,
    so_recv,
    st_send,
    st_recv,
    h_send,
    h_recv,
    m_send,
    m_recv,
    p_send,
    p_recv,
    e_send,
    e_recv,
    w_send,
    w_recv,
    g_send,
    g_recv,
):
    me = lax.axis_index("slab")
    tp = lax.axis_index("tp")
    core = lax.rem(me, 2)
    count_bits = slabs.bit_length() - 1
    groups = [(0, 1), (1, 1)] + [(b, min(2, count_bits - b)) for b in range(2, count_bits, 2)]
    stages = len(groups)
    tokens, width = tok_ref.shape
    cols, depth = ow_ref.shape
    heads = cols // HD
    planes = tokens // PLANE_TOK
    total = planes * slabs
    per_plane = PLANE_TOK // BLK
    pieces = PLANE_TOK // CHUNK
    halves = cols // 128
    last = planes - 1
    span = wsum.shape[0] // 2
    mine, theirs = part(tp, width), part(1 - tp, width)
    mate = {"tp": 1 - tp}
    slow = {"slab": lax.rem(me + slabs + 2 * core - 1, slabs)}
    fast = {"slab": me + 1 - 2 * core}
    sides = (slow, fast)
    sent = []

    def bit_of(b):
        return lax.rem(lax.div(me, 1 << b), 2)

    def digit_of(group, flip):
        first, size = group
        total_of = 0
        for n in range(size):
            bit = bit_of(first + n)
            total_of = total_of + ((1 - bit) if flip >> n & 1 else bit) * (1 << n)
        return total_of

    def peer(group, flip):
        return {"slab": me + (digit_of(group, flip) - digit_of(group, 0)) * (1 << group[0])}

    def peers(group):
        return [peer(group, flip) for flip in range(1, 1 << group[1])]

    def plane_of(k):
        return core * last + (1 - 2 * core) * k

    def nat(k, c, size=CHUNK):
        return pl.ds(pl.multiple_of(plane_of(k) * PLANE_TOK + c * size, size), size)

    def loc(k, c, size=CHUNK):
        return pl.ds(k * PLANE_TOK + c * size, size)

    barrier = pltpu.get_barrier_semaphore()
    greeted = [slow, mate] + [where for group in groups for where in peers(group)]
    for where in greeted:
        pl.semaphore_signal(barrier, inc=1, device_id=where, device_id_type=MESH)
    loads = {}
    for n, (name, src, dst) in enumerate(
        (
            ("tokens", tok_in, tok_ref),
            ("taps", taps_in_ref, taps_ref),
            ("key", wk_in, wk_ref),
            ("value", wv_in, wv_ref),
            ("query", wq_in, wq_ref),
            ("out", ow_in, ow_ref),
            ("cot", cot_in, cot_ref),
            ("blocks", blocks_in, blocks_ref),
            ("counts", counts_in, counts_ref),
        )
    ):
        loads[name] = pltpu.make_async_copy(src, dst, load_sem.at[n])
        loads[name].start()
    pl.semaphore_wait(barrier, len(greeted))

    def launch(copy):
        copy.start()
        sent.append(copy)
        return copy

    halos = {}
    for c in range(pieces):
        for side, k in ((0, 0), (1, last)):
            halos[side, c] = launch(
                copy_to(
                    tok_in.at[nat(k, c)], halo.at[side, loc(0, c)],
                    t_send.at[side, c], t_recv.at[side, c], sides[side],
                )
            )
    cots = {
        (k, c): copy_to(
            cot_in.at[nat(k, c)], ct.at[nat(k, c)],
            c_send.at[k * pieces + c], c_recv.at[k * pieces + c], mate,
        )
        for k in range(planes)
        for c in range(pieces)
    }
    waiting = list(cots)
    launch(cots[waiting.pop(0)])

    loads["tokens"].wait()
    loads["taps"].wait()
    tap_low = taps_ref[pl.ds(2 * core, 1), :]
    tap_mid = taps_ref[1:2, :]
    tap_high = taps_ref[pl.ds(2 - 2 * core, 1), :]

    def tokens_at(k, c):
        if k < 0:
            return halo[0, loc(0, c), :].astype(F32)
        if k > last:
            return halo[1, loc(0, c), :].astype(F32)
        return tok_ref[nat(k, c), :].astype(F32)

    def edges_of(k):
        return [(0, 0)] * (k == 0) + [(1, planes + 1)] * (k == last)

    order = [(k, c) for k in reversed(range(planes)) for c in range(pieces)]
    stems, so_halo, st_halo = {}, {}, {}
    for k, c in order:
        for side, _ in edges_of(k):
            halos[side, c].wait_recv()
        rows = loc(k + 1, c)
        so[rows, :] = (
            tap_low * tokens_at(k - 1, c) + tap_mid * tokens_at(k, c) + tap_high * tokens_at(k + 1, c)
        ).astype(BF16)
        stems[k, c] = launch(
            copy_to(
                so.at[rows], st.at[rows], s_send.at[k * pieces + c], s_recv.at[k * pieces + c], mate
            )
        )
        for side, e in edges_of(k):
            so_halo[side, c] = launch(
                copy_to(
                    so.at[rows], so.at[loc(e, c)],
                    so_send.at[side, c], so_recv.at[side, c], sides[side],
                )
            )

    def project(w_ref, rows):
        return (mm(so[rows, :], w_ref[mine, :]) + mm(st[rows, :], w_ref[theirs, :])).astype(BF16)

    def keys_values(rows):
        for half, w_ref in enumerate((wk_ref, wv_ref)):
            value = project(w_ref, rows)
            for n in range(CHUNK // BLK):
                kv[rows.start // BLK + n, :, half * cols : (half + 1) * cols] = value[
                    n * BLK : (n + 1) * BLK
                ]

    for name in ("key", "value", "query", "out", "cot", "blocks", "counts"):
        loads[name].wait()
    for n, (k, c) in enumerate(order):
        rows = loc(k + 1, c)
        stems[k, c].wait_recv()
        for side, e in edges_of(k):
            st_halo[side, c] = launch(
                copy_to(
                    st.at[rows], st.at[loc(e, c)],
                    st_send.at[side, c], st_recv.at[side, c], sides[side],
                )
            )
        if n == len(order) - 2:
            launch(cots[waiting.pop(0)])
        if n == len(order) - 1:
            for name in waiting:
                launch(cots[name])
        keys_values(rows)
        q[nat(k, c), :] = project(wq_ref, rows)

    def output_gradient(k):
        for c in range(pieces):
            rows = nat(k, c)
            cots[k, c].wait_recv()
            grad[rows, :] = (
                mm_nt(cot_ref[rows, :], ow_ref[:, mine]) + mm_nt(ct[rows, :], ow_ref[:, theirs])
            ).astype(BF16)

    def halo_keys(side, e):
        for c in range(pieces):
            so_halo[side, c].wait_recv()
            st_halo[side, c].wait_recv()
            keys_values(loc(e, c))

    halo_keys(1, planes + 1)
    output_gradient(0)
    halo_keys(0, 0)

    lane = lax.broadcasted_iota(jnp.int32, (1, cols), 1) // HD
    masks = [(lane == h).astype(F32).astype(BF16) for h in range(heads)]

    def stack(block):
        return jnp.concatenate([block * mask for mask in masks], axis=0)

    def pick(value):
        heads_t = [
            value[h * HD : (h + 1) * HD, h * BLK : (h + 1) * BLK] for h in range(heads)
        ]
        return jnp.concatenate(heads_t, axis=0).T

    def free_slot(k, j):
        block = blocks_ref[MAXK - 1, plane_of(k) * per_plane + j]
        plane = lax.rem(
            lax.div(block, per_plane) - me * planes - plane_of(k) + 1 + total, total
        )
        plane = k + core * 2 + (1 - 2 * core) * jnp.minimum(plane, 2)
        return plane * per_plane + lax.rem(block, per_plane)

    def attention(k):
        @pl.loop(0, per_plane)
        def _(j):
            rows = nat(k, j, BLK)
            places = [
                pl.ds(pl.multiple_of(e * PLANE_TOK + j * BLK, BLK), BLK) for e in range(k, k + 3)
            ]
            where = [e * per_plane + j for e in range(k, k + 3)] + [free_slot(k, j)]
            pairs = [kv[at] for at in where]
            keys = jnp.concatenate([pair[:, :cols] for pair in pairs], axis=0)
            values = jnp.concatenate([pair[:, cols:] for pair in pairs], axis=0)
            queries = stack(q[rows, :] * jnp.asarray(HD**-0.5, BF16))
            grads = stack(grad[rows, :])
            scores = mm_nt(keys, queries)
            left_out = MAXK - counts_ref[plane_of(k) * per_plane + j]
            fixed = (MAXK - 1) * BLK
            scores = jnp.concatenate(
                [scores[:fixed], scores[fixed:] + left_out.astype(F32) * NEG], axis=0
            )
            exps = jnp.exp(scores - jnp.max(scores, axis=0, keepdims=True))
            probs = exps * (1.0 / jnp.sum(exps, axis=0, keepdims=True))
            round_probs = probs.astype(BF16)
            attn[rows, :] = pick(mm_tn(values, round_probs)).astype(BF16)
            gprobs = mm_nt(values, grads)
            inner = jnp.sum(probs * gprobs, axis=0, keepdims=True)
            gscores = (probs * (gprobs - inner)).astype(BF16)
            at = pl.ds(pl.multiple_of(k * PLANE_TOK + j * BLK, BLK), BLK)
            gq_all[at, :] = (pick(mm_tn(keys, gscores)) * (HD**-0.5)).astype(BF16)
            gkeys = mm(gscores, queries)
            gvalues = mm(round_probs, grads)
            for n, place in enumerate(places):
                for half, g in enumerate((gkeys, gvalues)):
                    columns = slice(half * cols, (half + 1) * cols)
                    block = g[n * BLK : (n + 1) * BLK]
                    if k == 0 or n == 2:
                        acc[place, columns] = block
                    else:
                        acc[place, columns] += block
            spare[k * per_plane + j, :, 0:cols] = gkeys[fixed:]
            spare[k * per_plane + j, :, cols : 2 * cols] = gvalues[fixed:]

    def collect(e):
        @pl.loop(0, per_plane)
        def _(t):
            at = pl.ds(pl.multiple_of(e * PLANE_TOK + t * BLK, BLK), BLK)
            value = acc[at, :]
            for k in range(max(e - 2, 0), min(e, last) + 1):
                for step in range(1, per_plane):
                    j = lax.rem(t + step, per_plane)
                    off = free_slot(k, j) - (e * per_plane + t)
                    hit = (1 - jnp.minimum(off * off, 1)).astype(F32)
                    value = value + hit * spare[k * per_plane + j]
            if 1 <= e <= planes:
                acc[at, :] = value
            low[at, :] = value.astype(BF16)

    returns = {}

    def give_back(side, e):
        rows = loc(e, 0, PLANE_TOK)
        returns[side] = launch(
            copy_to(
                low.at[rows], from_halo.at[side], h_send.at[side], h_recv.at[side], sides[side]
            )
        )

    mixes = {}

    def mix_heads(k):
        rows = nat(k, 0, PLANE_TOK)
        mix_out[rows, :] = mm(attn[rows, :], ow_ref[:, theirs]).astype(BF16)
        mixes[k] = launch(
            copy_to(mix_out.at[rows], mix_in.at[rows], m_send.at[k], m_recv.at[k], mate)
        )
        mix[rows, :] = mm(attn[rows, :], ow_ref[:, mine])

    for k in range(planes):
        if k > 0:
            output_gradient(k)
        attention(k)
        if k == 0:
            collect(0)
            give_back(0, 0)
        if k == last:
            collect(planes + 1)
            give_back(1, planes + 1)
        mix_heads(k)

    orders = (groups[:1] + groups[2:] + groups[1:2], groups)
    sizes = []
    for order_of in orders:
        left = [span]
        for _, size in order_of:
            left.append(left[-1] >> size)
        sizes.append(left)
    lows = [jnp.int32(0), jnp.int32(span)]
    trail = [[], []]
    step_of = [0, 0]
    flight = [[], []]
    links = [0, 0]

    def rows_at(at, size):
        return pl.ds(pl.multiple_of(at, 16), size)

    def travel(t, src, dst, where):
        n = links[t]
        links[t] = n + 1
        flight[t].append(launch(copy_to(src, dst, w_send.at[t, n], w_recv.at[t, n], where)))

    def slot_of(t, k, flip):
        size = sizes[t][k + 1]
        return pl.ds(span - sizes[t][k] + (flip - 1) * size, size)

    def advance(t):
        k = step_of[t]
        if k > 2 * stages:
            return
        for copy in flight[t]:
            copy.wait_recv()
        flight[t] = []
        if 1 <= k <= stages:
            at = rows_at(lows[t], sizes[t][k])
            value = wsum[at, :]
            for flip in range(1, 1 << orders[t][k - 1][1]):
                value = value + incoming[t, slot_of(t, k - 1, flip), :].astype(F32)
            if k < stages:
                wsum[at, :] = value
            else:
                final[at, :] = value.astype(BF16)
        if k < stages:
            group, size = orders[t][k], sizes[t][k + 1]
            for flip in range(1, 1 << group[1]):
                slots = slot_of(t, k, flip)
                give = lows[t] + digit_of(group, flip) * size
                outgoing[t, slots, :] = wsum[rows_at(give, size), :].astype(BF16)
                travel(t, outgoing.at[t, slots], incoming.at[t, slots], peer(group, flip))
            lows[t] = lows[t] + digit_of(group, 0) * size
            trail[t].append(lows[t])
        elif k < 2 * stages:
            j = 2 * stages - 1 - k
            at = rows_at(trail[t][j], sizes[t][j + 1])
            for where in peers(orders[t][j]):
                travel(t, final.at[at], final.at[at], where)
        step_of[t] = k + 1

    def weight_gradient(base, rows, g):
        for index, s_ref in ((tp, so), (1 - tp, st)):
            product = mm_tn(s_ref[rows, :], g)
            for half in range(halves):
                at = pl.multiple_of(base + half * depth + index * width, 128)
                wsum[pl.ds(at, width), :] = product[:, half * 128 : (half + 1) * 128]

    block = depth * halves
    inside = slice(PLANE_TOK, PLANE_TOK + tokens)
    weight_gradient(0, inside, gq_all[...])
    for index, c_ref in ((tp, cot_ref), (1 - tp, ct)):
        product = mm_tn(attn[...], c_ref[...])
        for half in range(width // 128):
            wsum[pl.ds(pl.multiple_of(block + (index * (width // 128) + half) * cols, 128), cols), :] = (
                product[:, half * 128 : (half + 1) * 128]
            )
    advance(0)
    for e in range(1, planes + 1):
        collect(e)
    everything = slice(0, low.shape[0])
    weight_gradient(2 * block, everything, low[:, :cols])
    weight_gradient(3 * block, everything, low[:, cols:])
    advance(1)
    advance(0)
    for k in range(planes):
        for c in range(pieces):
            rows = loc(k, c)
            gq = gq_all[rows, :]
            own[rows, :] = mm_nt(gq, wq_ref[mine, :])
            other[rows, :] = mm_nt(gq, wq_ref[theirs, :])
    advance(1)
    parts = {}
    for k in range(planes):
        for side, _ in edges_of(k):
            returns[side].wait_recv()
        for c in range(pieces):
            rows = loc(k, c)
            value = acc[loc(k + 1, c), :]
            for side, _ in edges_of(k):
                value = value + from_halo[side, loc(0, c), :].astype(F32)
            value = value.astype(BF16)
            gk, gv = value[:, :cols], value[:, cols:]
            part_out[rows, :] = (
                other[rows, :] + mm_nt(gk, wk_ref[theirs, :]) + mm_nt(gv, wv_ref[theirs, :])
            ).astype(BF16)
            parts[k, c] = launch(
                copy_to(
                    part_out.at[rows], part_in.at[rows],
                    p_send.at[k * pieces + c], p_recv.at[k * pieces + c], mate,
                )
            )
            own[rows, :] += mm_nt(gk, wk_ref[mine, :]) + mm_nt(gv, wv_ref[mine, :])
        advance(0)
        advance(1)
    for k in range(planes):
        rows = nat(k, 0, PLANE_TOK)
        mixes[k].wait_recv()
        layer_ref[rows, :] = (
            so[loc(k + 1, 0, PLANE_TOK), :].astype(F32) + (mix[rows, :] + mix_in[rows, :].astype(F32))
        ).astype(BF16)
    advance(0)
    advance(1)
    edges = {}
    for k in range(planes):
        for c in range(pieces):
            rows = loc(k, c)
            parts[k, c].wait_recv()
            stem_grad = cot_ref[nat(k, c), :].astype(F32) + (
                own[rows, :] + part_in[rows, :].astype(F32)
            )
            own[rows, :] = stem_grad
            for side, _ in edges_of(k):
                at = loc(side, c)
                edge[at, :] = stem_grad.astype(BF16)
                edges[side, c] = launch(
                    copy_to(
                        edge.at[at], edge_in.at[at],
                        e_send.at[side, c], e_recv.at[side, c], sides[side],
                    )
                )
        advance(0)
        advance(1)
    sums = [jnp.zeros((1, width), F32) for _ in range(3)]
    for k in range(planes):
        for c in range(pieces):
            g = own[loc(k, c), :]
            for n in range(3):
                sums[n] = sums[n] + jnp.sum(g * tokens_at(k - 1 + n, c), axis=0, keepdims=True)
    swap = core == 1
    sums = [jnp.where(swap, sums[2], sums[0]), sums[1], jnp.where(swap, sums[0], sums[2])]
    taps_sum[0] = jnp.concatenate(sums + [jnp.zeros((5, width), F32)], axis=0)

    def send_taps(k):
        base = sum((1 << size) - 1 for _, size in groups[:k])
        return [
            launch(
                copy_to(
                    taps_sum.at[k], taps_in.at[base + n],
                    g_send.at[base + n], g_recv.at[base + n], where,
                )
            )
            for n, where in enumerate(peers(groups[k]))
        ]

    def take_taps(k, copies):
        base = sum((1 << size) - 1 for _, size in groups[:k])
        value = taps_sum[k]
        for n, copy in enumerate(copies):
            copy.wait_recv()
            value = value + taps_in[base + n]
        taps_sum[k + 1] = value

    def gradient_at(k, c):
        if k < 0:
            return edge_in[loc(0, c), :].astype(F32)
        if k > last:
            return edge_in[loc(1, c), :].astype(F32)
        return own[loc(k, c), :]

    def finish_tokens():
        for copy in edges.values():
            copy.wait_recv()
        for k in range(planes):
            for c in range(pieces):
                grad_ref[nat(k, c), :] = (
                    tap_low * gradient_at(k + 1, c) + tap_mid * gradient_at(k, c)
                    + tap_high * gradient_at(k - 1, c)
                )

    for k in range(stages):
        copy = send_taps(k)
        advance(1)
        advance(0)
        if k == 0:
            finish_tokens()
        take_taps(k, copy)
    for _ in range(2 * stages):
        advance(0)
        advance(1)
    taps_out_ref[...] = taps_sum[stages]
    for copy in sent:
        copy.wait_send()


def unpack_kernel(
    final_ref, taps_in_ref, layer_in, grad_in, gqw_ref, gkw_ref, gvw_ref, go_ref, taps_ref,
    layer_ref, grad_ref, gqw, gkw, gvw, go, taps, sem,
):
    copies = [
        pltpu.make_async_copy(grad_in, grad_ref, sem.at[0]),
        pltpu.make_async_copy(layer_in, layer_ref, sem.at[1]),
    ]
    for copy in copies:
        copy.start()
    at = 0
    for n, (out, dst) in enumerate(((gqw, gqw_ref), (go, go_ref), (gkw, gkw_ref), (gvw, gvw_ref))):
        rows = out.shape[0]
        for half in range(out.shape[1] // 128):
            out[:, half * 128 : (half + 1) * 128] = final_ref[at : at + rows, :].astype(F32)
            at += rows
        copies.append(pltpu.make_async_copy(out, dst, sem.at[2 + n]))
        copies[-1].start()
    taps[...] = taps_in_ref[0:3, :]
    copies.append(pltpu.make_async_copy(taps, taps_ref, sem.at[6]))
    copies[-1].start()
    for copy in copies:
        copy.wait()


def body(
    slabs,
    tokens,
    stem_taps,
    query_weight,
    key_weight,
    value_weight,
    out_weight,
    key_blocks,
    counts,
    cotangent,
):
    count, width = tokens.shape
    depth, cols = query_weight.shape
    plane = PLANE_TOK
    planes = count // plane
    sds = jax.ShapeDtypeStruct
    params = pltpu.CompilerParams(vmem_limit_bytes=20 * MIB)
    count_bits = slabs.bit_length() - 1
    radix = [2, 2] + [1 << min(2, count_bits - b) for b in range(2, count_bits, 2)]
    stages = len(radix)
    links = sum(radix) - stages
    chunks = count // CHUNK
    pieces = plane // CHUNK
    blocks = count // BLK
    wide = count + 2 * plane
    dma = pltpu.SemaphoreType.DMA
    rows = 4 * depth * cols // 128
    semaphores = [
        (2, pieces),
        (chunks,),
        (chunks,),
        (2, pieces),
        (2, pieces),
        (2,),
        (planes,),
        (chunks,),
        (2, pieces),
        (2, 2 * links),
        (links,),
    ]
    layer_out, grad_tokens, final, taps = pl.pallas_call(
        functools.partial(layer_kernel, slabs),
        out_shape=[
            sds((count, width), BF16),
            sds((count, width), F32),
            sds((rows, 128), BF16),
            sds((8, width), F32),
        ],
        in_specs=[HBM] * 9,
        out_specs=[VMEM] * 4,
        scratch_shapes=[
            pltpu.SMEM((MAXK, blocks), jnp.int32),
            pltpu.SMEM((blocks,), jnp.int32),
            pltpu.VMEM((count, width), BF16),
            pltpu.VMEM((count, width), BF16),
            pltpu.VMEM(stem_taps.shape, F32),
            pltpu.VMEM((depth, cols), BF16),
            pltpu.VMEM((depth, cols), BF16),
            pltpu.VMEM((depth, cols), BF16),
            pltpu.VMEM((cols, depth), BF16),
            dma((9,)),
            pltpu.VMEM((2, plane, width), BF16),
            pltpu.VMEM((wide, width), BF16),
            pltpu.VMEM((wide, width), BF16),
            pltpu.VMEM((count, width), BF16),
            pltpu.VMEM((count, cols), BF16),
            pltpu.VMEM((wide // BLK, BLK, 2 * cols), BF16),
            pltpu.VMEM((count, cols), BF16),
            pltpu.VMEM((count, cols), BF16),
            pltpu.VMEM((wide, 2 * cols), F32),
            pltpu.VMEM((blocks, BLK, 2 * cols), F32),
            pltpu.VMEM((count, cols), BF16),
            pltpu.VMEM((wide, 2 * cols), BF16),
            pltpu.VMEM((2, plane, 2 * cols), BF16),
            pltpu.VMEM((count, width), F32),
            pltpu.VMEM((count, width), BF16),
            pltpu.VMEM((count, width), BF16),
            pltpu.VMEM((count, width), F32),
            pltpu.VMEM((count, width), F32),
            pltpu.VMEM((count, width), BF16),
            pltpu.VMEM((count, width), BF16),
            pltpu.VMEM((2 * plane, width), BF16),
            pltpu.VMEM((2 * plane, width), BF16),
            pltpu.VMEM((rows, 128), F32),
            pltpu.VMEM((2, rows // 2, 128), BF16),
            pltpu.VMEM((2, rows // 2, 128), BF16),
            pltpu.VMEM((links, 8, width), F32),
            pltpu.VMEM((stages + 1, 8, width), F32),
        ]
        + [dma(shape) for shape in semaphores for _ in range(2)],
        compiler_params=pltpu.CompilerParams(
            collective_id=0, has_side_effects=True, vmem_limit_bytes=44 * MIB
        ),
    )(
        key_blocks.T,
        counts,
        tokens,
        cotangent,
        stem_taps,
        query_weight,
        key_weight,
        value_weight,
        out_weight,
    )
    weight = sds((depth, cols), F32)
    out_grad = sds((cols, depth), F32)
    tap_grad = sds(stem_taps.shape, F32)
    gqw, gkw, gvw, go, grad_taps, layer_out, grad_tokens = pl.pallas_call(
        unpack_kernel,
        out_shape=[
            weight, weight, weight, out_grad, tap_grad,
            sds((count, width), BF16), sds((count, width), F32),
        ],
        in_specs=[VMEM] * 4,
        out_specs=[HBM] * 7,
        scratch_shapes=[
            pltpu.VMEM(s.shape, F32) for s in (weight, weight, weight, out_grad, tap_grad)
        ]
        + [dma((7,))],
        compiler_params=params,
    )(final, taps, layer_out, grad_tokens)
    return (layer_out, grad_tokens, grad_taps, gqw, gkw, gvw, go)


def solution(mesh):
    in_specs = (
        P("slab", "tp"),
        P(None, "tp"),
        P(None, "tp"),
        P(None, "tp"),
        P(None, "tp"),
        P("tp", None),
        P("slab", None),
        P("slab"),
        P("slab", "tp"),
    )
    out_specs = (
        P("slab", "tp"),
        P("slab", "tp"),
        P(None, "tp"),
        P(None, "tp"),
        P(None, "tp"),
        P(None, "tp"),
        P("tp", None),
    )
    return jax.shard_map(
        functools.partial(body, mesh.shape["slab"]),
        mesh=mesh,
        in_specs=in_specs,
        out_specs=out_specs,
        check_vma=False,
    )
```

```python
import functools

import jax
import jax.numpy as jnp
from jax import lax
from jax.experimental import pallas as pl
from jax.experimental.pallas import tpu as pltpu
from jax.sharding import PartitionSpec as P

HD = 64
BLK = 128
PLANE_TOK = 512
MAXK = 4
NEG = -1e30
F32 = jnp.float32
BF16 = jnp.bfloat16
MESH = pl.DeviceIdType.MESH
HBM = pl.BlockSpec(memory_space=pltpu.HBM)
MIB = 1024 * 1024
CHUNK = 256


def mm(a, b):
    return jnp.dot(a, b, preferred_element_type=F32)


def mm_nt(a, b):
    return lax.dot_general(a, b, (((1,), (1,)), ((), ())), preferred_element_type=F32)


def mm_tn(a, b):
    return lax.dot_general(a, b, (((0,), (0,)), ((), ())), preferred_element_type=F32)


def part(index, width):
    return pl.ds(pl.multiple_of(index * width, width), width)


def copy_to(src, dst, send, recv, where):
    return pltpu.make_async_remote_copy(
        src_ref=src,
        dst_ref=dst,
        send_sem=send,
        recv_sem=recv,
        device_id=where,
        device_id_type=MESH,
    )


def layer_kernel(
    slabs,
    blocks_in,
    counts_in,
    tok_in,
    cot_in,
    taps_in_ref,
    wq_in,
    wk_in,
    wv_in,
    ow_in,
    layer_out_ref,
    grad_out_ref,
    final_out_ref,
    taps_out_ref,
    blocks_ref,
    counts_ref,
    tok_ref,
    cot_ref,
    taps_ref,
    wq_ref,
    wk_ref,
    wv_ref,
    ow_ref,
    layer_ref,
    grad_ref,
    final,
    load_sem,
    store_sem,
    halo,
    so,
    st,
    ct,
    q,
    kv,
    grad,
    attn,
    acc,
    spare,
    gq_all,
    low,
    from_halo,
    mix,
    mix_out,
    mix_in,
    own,
    other,
    part_out,
    part_in,
    edge,
    edge_in,
    wsum,
    outgoing,
    incoming,
    taps_in,
    taps_sum,
    t_send,
    t_recv,
    s_send,
    s_recv,
    c_send,
    c_recv,
    so_send,
    so_recv,
    st_send,
    st_recv,
    h_send,
    h_recv,
    m_send,
    m_recv,
    p_send,
    p_recv,
    e_send,
    e_recv,
    w_send,
    w_recv,
    g_send,
    g_recv,
):
    me = lax.axis_index("slab")
    tp = lax.axis_index("tp")
    core = lax.rem(me, 2)
    count_bits = slabs.bit_length() - 1
    groups = [(0, 1), (1, 1)] + [(b, min(2, count_bits - b)) for b in range(2, count_bits, 2)]
    tap_groups = [(0, 1)] + [(b, min(3, count_bits - b)) for b in range(1, count_bits, 3)]
    stages = len(groups)
    tokens, width = tok_ref.shape
    cols, depth = ow_ref.shape
    heads = cols // HD
    planes = tokens // PLANE_TOK
    total = planes * slabs
    per_plane = PLANE_TOK // BLK
    pieces = PLANE_TOK // CHUNK
    halves = cols // 128
    last = planes - 1
    span = wsum.shape[0] // 2
    mine, theirs = part(tp, width), part(1 - tp, width)
    mate = {"tp": 1 - tp}
    slow = {"slab": lax.rem(me + slabs + 2 * core - 1, slabs)}
    fast = {"slab": me + 1 - 2 * core}
    sides = (slow, fast)
    sent = []

    def bit_of(b):
        return lax.rem(lax.div(me, 1 << b), 2)

    def digit_of(group, flip):
        first, size = group
        total_of = 0
        for n in range(size):
            bit = bit_of(first + n)
            total_of = total_of + ((1 - bit) if flip >> n & 1 else bit) * (1 << n)
        return total_of

    def peer_at(flip):
        move = 0
        for b in range(count_bits):
            if flip >> b & 1:
                move = move + (1 - 2 * bit_of(b)) * (1 << b)
        return {"slab": me + move}

    def peer(group, flip):
        return peer_at(flip << group[0])

    def peers(group):
        return [peer(group, flip) for flip in range(1, 1 << group[1])]

    def plane_of(k):
        return core * last + (1 - 2 * core) * k

    def nat(k, c, size=CHUNK):
        return pl.ds(pl.multiple_of(plane_of(k) * PLANE_TOK + c * size, size), size)

    def loc(k, c, size=CHUNK):
        return pl.ds(k * PLANE_TOK + c * size, size)

    barrier = pltpu.get_barrier_semaphore()
    flips = {
        flip << group[0] for group in groups + tap_groups for flip in range(1, 1 << group[1])
    }
    greeted = [slow, mate] + [peer_at(flip) for flip in sorted(flips)]
    for where in greeted:
        pl.semaphore_signal(barrier, inc=1, device_id=where, device_id_type=MESH)
    loads = {}
    for n, (name, src, dst) in enumerate(
        (
            ("tokens", tok_in, tok_ref),
            ("taps", taps_in_ref, taps_ref),
            ("key", wk_in, wk_ref),
            ("value", wv_in, wv_ref),
            ("query", wq_in, wq_ref),
            ("out", ow_in, ow_ref),
            ("cot", cot_in, cot_ref),
            ("blocks", blocks_in, blocks_ref),
            ("counts", counts_in, counts_ref),
        )
    ):
        loads[name] = pltpu.make_async_copy(src, dst, load_sem.at[n])
        loads[name].start()
    pl.semaphore_wait(barrier, len(greeted))

    def launch(copy):
        copy.start()
        sent.append(copy)
        return copy

    halos = {}
    for c in range(pieces):
        for side, k in ((0, 0), (1, last)):
            halos[side, c] = launch(
                copy_to(
                    tok_in.at[nat(k, c)], halo.at[side, loc(0, c)],
                    t_send.at[side, c], t_recv.at[side, c], sides[side],
                )
            )
    cots = {
        (k, c): copy_to(
            cot_in.at[nat(k, c)], ct.at[nat(k, c)],
            c_send.at[k * pieces + c], c_recv.at[k * pieces + c], mate,
        )
        for k in range(planes)
        for c in range(pieces)
    }
    waiting = list(cots)
    launch(cots[waiting.pop(0)])

    loads["tokens"].wait()
    loads["taps"].wait()
    tap_low = taps_ref[pl.ds(2 * core, 1), :]
    tap_mid = taps_ref[1:2, :]
    tap_high = taps_ref[pl.ds(2 - 2 * core, 1), :]

    def tokens_at(k, c):
        if k < 0:
            return halo[0, loc(0, c), :].astype(F32)
        if k > last:
            return halo[1, loc(0, c), :].astype(F32)
        return tok_ref[nat(k, c), :].astype(F32)

    def edges_of(k):
        return [(0, 0)] * (k == 0) + [(1, planes + 1)] * (k == last)

    order = [(k, c) for k in reversed(range(planes)) for c in range(pieces)]
    stems, so_halo, st_halo = {}, {}, {}
    for k, c in order:
        for side, _ in edges_of(k):
            halos[side, c].wait_recv()
        rows = loc(k + 1, c)
        so[rows, :] = (
            tap_low * tokens_at(k - 1, c) + tap_mid * tokens_at(k, c) + tap_high * tokens_at(k + 1, c)
        ).astype(BF16)
        stems[k, c] = launch(
            copy_to(
                so.at[rows], st.at[rows], s_send.at[k * pieces + c], s_recv.at[k * pieces + c], mate
            )
        )
        for side, e in edges_of(k):
            so_halo[side, c] = launch(
                copy_to(
                    so.at[rows], so.at[loc(e, c)],
                    so_send.at[side, c], so_recv.at[side, c], sides[side],
                )
            )

    def project(w_ref, rows):
        return (mm(so[rows, :], w_ref[mine, :]) + mm(st[rows, :], w_ref[theirs, :])).astype(BF16)

    def keys_values(rows):
        for half, w_ref in enumerate((wk_ref, wv_ref)):
            value = project(w_ref, rows)
            for n in range(CHUNK // BLK):
                kv[rows.start // BLK + n, :, half * cols : (half + 1) * cols] = value[
                    n * BLK : (n + 1) * BLK
                ]

    for name in ("key", "value", "query", "out", "cot", "blocks", "counts"):
        loads[name].wait()
    for n, (k, c) in enumerate(order):
        rows = loc(k + 1, c)
        stems[k, c].wait_recv()
        for side, e in edges_of(k):
            st_halo[side, c] = launch(
                copy_to(
                    st.at[rows], st.at[loc(e, c)],
                    st_send.at[side, c], st_recv.at[side, c], sides[side],
                )
            )
        if n == len(order) - 2:
            launch(cots[waiting.pop(0)])
        if n == len(order) - 1:
            for name in waiting:
                launch(cots[name])
        keys_values(rows)
        q[nat(k, c), :] = project(wq_ref, rows)

    def output_gradient(k):
        for c in range(pieces):
            rows = nat(k, c)
            cots[k, c].wait_recv()
            grad[rows, :] = (
                mm_nt(cot_ref[rows, :], ow_ref[:, mine]) + mm_nt(ct[rows, :], ow_ref[:, theirs])
            ).astype(BF16)

    def halo_keys(side, e):
        for c in range(pieces):
            so_halo[side, c].wait_recv()
            st_halo[side, c].wait_recv()
            keys_values(loc(e, c))

    halo_keys(1, planes + 1)
    output_gradient(0)
    halo_keys(0, 0)

    lane = lax.broadcasted_iota(jnp.int32, (1, cols), 1) // HD
    masks = [(lane == h).astype(F32).astype(BF16) for h in range(heads)]

    def stack(block):
        return jnp.concatenate([block * mask for mask in masks], axis=0)

    def pick(value):
        heads_t = [
            value[h * HD : (h + 1) * HD, h * BLK : (h + 1) * BLK] for h in range(heads)
        ]
        return jnp.concatenate(heads_t, axis=0).T

    def free_slot(k, j):
        block = blocks_ref[MAXK - 1, plane_of(k) * per_plane + j]
        plane = lax.rem(
            lax.div(block, per_plane) - me * planes - plane_of(k) + 1 + total, total
        )
        plane = k + core * 2 + (1 - 2 * core) * jnp.minimum(plane, 2)
        return plane * per_plane + lax.rem(block, per_plane)

    def attention(k):
        @pl.loop(0, per_plane)
        def _(j):
            rows = nat(k, j, BLK)
            places = [
                pl.ds(pl.multiple_of(e * PLANE_TOK + j * BLK, BLK), BLK) for e in range(k, k + 3)
            ]
            where = [e * per_plane + j for e in range(k, k + 3)] + [free_slot(k, j)]
            pairs = [kv[at] for at in where]
            keys = jnp.concatenate([pair[:, :cols] for pair in pairs], axis=0)
            values = jnp.concatenate([pair[:, cols:] for pair in pairs], axis=0)
            queries = stack(q[rows, :] * jnp.asarray(HD**-0.5, BF16))
            grads = stack(grad[rows, :])
            scores = mm_nt(keys, queries)
            left_out = MAXK - counts_ref[plane_of(k) * per_plane + j]
            fixed = (MAXK - 1) * BLK
            scores = jnp.concatenate(
                [scores[:fixed], scores[fixed:] + left_out.astype(F32) * NEG], axis=0
            )
            exps = jnp.exp(scores - jnp.max(scores, axis=0, keepdims=True))
            probs = exps * (1.0 / jnp.sum(exps, axis=0, keepdims=True))
            round_probs = probs.astype(BF16)
            attn[rows, :] = pick(mm_tn(values, round_probs)).astype(BF16)
            gprobs = mm_nt(values, grads)
            inner = jnp.sum(probs * gprobs, axis=0, keepdims=True)
            gscores = (probs * (gprobs - inner)).astype(BF16)
            at = pl.ds(pl.multiple_of(k * PLANE_TOK + j * BLK, BLK), BLK)
            gq_all[at, :] = (pick(mm_tn(keys, gscores)) * (HD**-0.5)).astype(BF16)
            gkeys = mm(gscores, queries)
            gvalues = mm(round_probs, grads)
            for n, place in enumerate(places):
                for half, g in enumerate((gkeys, gvalues)):
                    columns = slice(half * cols, (half + 1) * cols)
                    block = g[n * BLK : (n + 1) * BLK]
                    if k == 0 or n == 2:
                        acc[place, columns] = block
                    else:
                        acc[place, columns] += block
            spare[k * per_plane + j, :, 0:cols] = gkeys[fixed:]
            spare[k * per_plane + j, :, cols : 2 * cols] = gvalues[fixed:]

    def collect(e):
        @pl.loop(0, per_plane)
        def _(t):
            at = pl.ds(pl.multiple_of(e * PLANE_TOK + t * BLK, BLK), BLK)
            value = acc[at, :]
            for k in range(max(e - 2, 0), min(e, last) + 1):
                for step in range(1, per_plane):
                    j = lax.rem(t + step, per_plane)
                    off = free_slot(k, j) - (e * per_plane + t)
                    hit = (1 - jnp.minimum(off * off, 1)).astype(F32)
                    value = value + hit * spare[k * per_plane + j]
            if 1 <= e <= planes:
                acc[at, :] = value
            low[at, :] = value.astype(BF16)

    returns = {}

    def give_back(side, e):
        rows = loc(e, 0, PLANE_TOK)
        returns[side] = launch(
            copy_to(
                low.at[rows], from_halo.at[side], h_send.at[side], h_recv.at[side], sides[side]
            )
        )

    mixes = {}

    def mix_heads(k):
        rows = nat(k, 0, PLANE_TOK)
        mix_out[rows, :] = mm(attn[rows, :], ow_ref[:, theirs]).astype(BF16)
        mixes[k] = launch(
            copy_to(mix_out.at[rows], mix_in.at[rows], m_send.at[k], m_recv.at[k], mate)
        )
        mix[rows, :] = mm(attn[rows, :], ow_ref[:, mine])

    for k in range(planes):
        if k > 0:
            output_gradient(k)
        attention(k)
        if k == 0:
            collect(0)
            give_back(0, 0)
        if k == last:
            collect(planes + 1)
            give_back(1, planes + 1)
        mix_heads(k)

    orders = (groups[:1] + groups[2:] + groups[1:2], groups)
    sizes = []
    for order_of in orders:
        left = [span]
        for _, size in order_of:
            left.append(left[-1] >> size)
        sizes.append(left)
    lows = [jnp.int32(0), jnp.int32(span)]
    trail = [[], []]
    step_of = [0, 0]
    flight = [[], []]
    links = [0, 0]

    def rows_at(at, size):
        return pl.ds(pl.multiple_of(at, 16), size)

    def travel(t, src, dst, where):
        n = links[t]
        links[t] = n + 1
        flight[t].append(launch(copy_to(src, dst, w_send.at[t, n], w_recv.at[t, n], where)))

    def slot_of(t, k, flip):
        size = sizes[t][k + 1]
        return pl.ds(span - sizes[t][k] + (flip - 1) * size, size)

    def advance(t):
        k = step_of[t]
        if k > 2 * stages:
            return
        for copy in flight[t]:
            copy.wait_recv()
        flight[t] = []
        if 1 <= k <= stages:
            at = rows_at(lows[t], sizes[t][k])
            value = wsum[at, :]
            for flip in range(1, 1 << orders[t][k - 1][1]):
                value = value + incoming[t, slot_of(t, k - 1, flip), :].astype(F32)
            if k < stages:
                wsum[at, :] = value
            else:
                final[at, :] = value.astype(BF16)
        if k < stages:
            group, size = orders[t][k], sizes[t][k + 1]
            for flip in range(1, 1 << group[1]):
                slots = slot_of(t, k, flip)
                give = lows[t] + digit_of(group, flip) * size
                outgoing[t, slots, :] = wsum[rows_at(give, size), :].astype(BF16)
                travel(t, outgoing.at[t, slots], incoming.at[t, slots], peer(group, flip))
            lows[t] = lows[t] + digit_of(group, 0) * size
            trail[t].append(lows[t])
        elif k < 2 * stages:
            j = 2 * stages - 1 - k
            at = rows_at(trail[t][j], sizes[t][j + 1])
            for where in peers(orders[t][j]):
                travel(t, final.at[at], final.at[at], where)
        step_of[t] = k + 1

    def weight_gradient(base, rows, g):
        for index, s_ref in ((tp, so), (1 - tp, st)):
            product = mm_tn(s_ref[rows, :], g)
            for half in range(halves):
                at = pl.multiple_of(base + half * depth + index * width, 128)
                wsum[pl.ds(at, width), :] = product[:, half * 128 : (half + 1) * 128]

    block = depth * halves
    inside = slice(PLANE_TOK, PLANE_TOK + tokens)
    weight_gradient(0, inside, gq_all[...])
    for index, c_ref in ((tp, cot_ref), (1 - tp, ct)):
        product = mm_tn(attn[...], c_ref[...])
        for half in range(width // 128):
            wsum[pl.ds(pl.multiple_of(block + (index * (width // 128) + half) * cols, 128), cols), :] = (
                product[:, half * 128 : (half + 1) * 128]
            )
    advance(0)
    for e in range(1, planes + 1):
        collect(e)
    everything = slice(0, low.shape[0])
    weight_gradient(2 * block, everything, low[:, :cols])
    weight_gradient(3 * block, everything, low[:, cols:])
    advance(1)
    advance(0)
    for k in range(planes):
        for c in range(pieces):
            rows = loc(k, c)
            gq = gq_all[rows, :]
            own[rows, :] = mm_nt(gq, wq_ref[mine, :])
            other[rows, :] = mm_nt(gq, wq_ref[theirs, :])
    parts = {}
    for k in range(planes):
        for side, _ in edges_of(k):
            returns[side].wait_recv()
        for c in range(pieces):
            rows = loc(k, c)
            value = acc[loc(k + 1, c), :]
            for side, _ in edges_of(k):
                value = value + from_halo[side, loc(0, c), :].astype(F32)
            value = value.astype(BF16)
            gk, gv = value[:, :cols], value[:, cols:]
            part_out[rows, :] = (
                other[rows, :] + mm_nt(gk, wk_ref[theirs, :]) + mm_nt(gv, wv_ref[theirs, :])
            ).astype(BF16)
            parts[k, c] = launch(
                copy_to(
                    part_out.at[rows], part_in.at[rows],
                    p_send.at[k * pieces + c], p_recv.at[k * pieces + c], mate,
                )
            )
            own[rows, :] += mm_nt(gk, wk_ref[mine, :]) + mm_nt(gv, wv_ref[mine, :])
        if k == 0:
            advance(1)
    for k in range(planes):
        rows = nat(k, 0, PLANE_TOK)
        mixes[k].wait_recv()
        layer_ref[rows, :] = (
            so[loc(k + 1, 0, PLANE_TOK), :].astype(F32) + (mix[rows, :] + mix_in[rows, :].astype(F32))
        ).astype(BF16)
    stores = [pltpu.make_async_copy(layer_ref, layer_out_ref, store_sem.at[0])]
    stores[0].start()
    edges = {}
    sums = [jnp.zeros((1, width), F32) for _ in range(3)]
    turns = [1, 0, 0, 1, 0]
    for k in range(planes):
        for c in range(pieces):
            rows = loc(k, c)
            parts[k, c].wait_recv()
            stem_grad = cot_ref[nat(k, c), :].astype(F32) + (
                own[rows, :] + part_in[rows, :].astype(F32)
            )
            own[rows, :] = stem_grad
            for side, _ in edges_of(k):
                at = loc(side, c)
                edge[at, :] = stem_grad.astype(BF16)
                edges[side, c] = launch(
                    copy_to(
                        edge.at[at], edge_in.at[at],
                        e_send.at[side, c], e_recv.at[side, c], sides[side],
                    )
                )
            for n in range(3):
                sums[n] = sums[n] + jnp.sum(
                    stem_grad * tokens_at(k - 1 + n, c), axis=0, keepdims=True
                )
            if turns and (k, c) != (last, pieces - 1):
                advance(turns.pop(0))
    swap = core == 1
    sums = [jnp.where(swap, sums[2], sums[0]), sums[1], jnp.where(swap, sums[0], sums[2])]
    taps_sum[0] = jnp.concatenate(sums + [jnp.zeros((5, width), F32)], axis=0)

    def send_taps(k):
        base = sum((1 << size) - 1 for _, size in tap_groups[:k])
        return [
            launch(
                copy_to(
                    taps_sum.at[k], taps_in.at[base + n],
                    g_send.at[base + n], g_recv.at[base + n], where,
                )
            )
            for n, where in enumerate(peers(tap_groups[k]))
        ]

    def take_taps(k, copies):
        base = sum((1 << size) - 1 for _, size in tap_groups[:k])
        value = taps_sum[k]
        for n, copy in enumerate(copies):
            copy.wait_recv()
            value = value + taps_in[base + n]
        taps_sum[k + 1] = value

    def gradient_at(k, c):
        if k < 0:
            return edge_in[loc(0, c), :].astype(F32)
        if k > last:
            return edge_in[loc(1, c), :].astype(F32)
        return own[loc(k, c), :]

    def finish_tokens():
        for copy in edges.values():
            copy.wait_recv()
        for k in range(planes):
            for c in range(pieces):
                grad_ref[nat(k, c), :] = (
                    tap_low * gradient_at(k + 1, c) + tap_mid * gradient_at(k, c)
                    + tap_high * gradient_at(k - 1, c)
                )
        stores.append(pltpu.make_async_copy(grad_ref, grad_out_ref, store_sem.at[1]))
        stores[-1].start()

    for k in range(len(tap_groups)):
        copies = send_taps(k)
        advance(0)
        advance(1)
        if k == 0:
            finish_tokens()
        take_taps(k, copies)
    for _ in range(2 * stages):
        advance(0)
        advance(1)
    stores.append(pltpu.make_async_copy(final, final_out_ref, store_sem.at[2]))
    stores.append(
        pltpu.make_async_copy(taps_sum.at[len(tap_groups)], taps_out_ref, store_sem.at[3])
    )
    for store in stores[-2:]:
        store.start()
    for store in stores:
        store.wait()
    for copy in sent:
        copy.wait_send()


def unpack_kernel(
    final_in, taps_in, layer_in, grad_in, gqw_ref, gkw_ref, gvw_ref, go_ref, taps_ref,
    layer_ref, grad_ref, final_ref, gqw, gkw, gvw, go, load_sem, sem,
):
    copies = [
        pltpu.make_async_copy(grad_in, grad_ref, sem.at[0]),
        pltpu.make_async_copy(layer_in, layer_ref, sem.at[1]),
        pltpu.make_async_copy(taps_in.at[0 : taps_ref.shape[0]], taps_ref, sem.at[2]),
    ]
    outs = ((gqw, gqw_ref), (go, go_ref), (gkw, gkw_ref), (gvw, gvw_ref))
    part_rows = final_ref.shape[0] // len(outs)
    loads = [
        pltpu.make_async_copy(final_in.at[at], final_ref.at[at], load_sem.at[n])
        for n, at in enumerate(pl.ds(n * part_rows, part_rows) for n in range(len(outs)))
    ]
    for copy in loads + copies:
        copy.start()
    at = 0
    for n, (out, dst) in enumerate(outs):
        loads[n].wait()
        rows = out.shape[0]
        for half in range(out.shape[1] // 128):
            out[:, half * 128 : (half + 1) * 128] = final_ref[at : at + rows, :].astype(F32)
            at += rows
        copies.append(pltpu.make_async_copy(out, dst, sem.at[3 + n]))
        copies[-1].start()
    for copy in copies:
        copy.wait()


def body(
    slabs,
    tokens,
    stem_taps,
    query_weight,
    key_weight,
    value_weight,
    out_weight,
    key_blocks,
    counts,
    cotangent,
):
    count, width = tokens.shape
    depth, cols = query_weight.shape
    plane = PLANE_TOK
    planes = count // plane
    sds = jax.ShapeDtypeStruct
    count_bits = slabs.bit_length() - 1
    radix = [2, 2] + [1 << min(2, count_bits - b) for b in range(2, count_bits, 2)]
    links = sum(radix) - len(radix)
    tap_radix = [2] + [1 << min(3, count_bits - b) for b in range(1, count_bits, 3)]
    tap_links = sum(tap_radix) - len(tap_radix)
    chunks = count // CHUNK
    pieces = plane // CHUNK
    blocks = count // BLK
    wide = count + 2 * plane
    dma = pltpu.SemaphoreType.DMA
    rows = 4 * depth * cols // 128
    semaphores = [
        (2, pieces),
        (chunks,),
        (chunks,),
        (2, pieces),
        (2, pieces),
        (2,),
        (planes,),
        (chunks,),
        (2, pieces),
        (2, 2 * links),
        (tap_links,),
    ]
    layer_out, grad_tokens, final, taps = pl.pallas_call(
        functools.partial(layer_kernel, slabs),
        out_shape=[
            sds((count, width), BF16),
            sds((count, width), F32),
            sds((rows, 128), BF16),
            sds((8, width), F32),
        ],
        in_specs=[HBM] * 9,
        out_specs=[HBM] * 4,
        scratch_shapes=[
            pltpu.SMEM((MAXK, blocks), jnp.int32),
            pltpu.SMEM((blocks,), jnp.int32),
            pltpu.VMEM((count, width), BF16),
            pltpu.VMEM((count, width), BF16),
            pltpu.VMEM(stem_taps.shape, F32),
            pltpu.VMEM((depth, cols), BF16),
            pltpu.VMEM((depth, cols), BF16),
            pltpu.VMEM((depth, cols), BF16),
            pltpu.VMEM((cols, depth), BF16),
            pltpu.VMEM((count, width), BF16),
            pltpu.VMEM((count, width), F32),
            pltpu.VMEM((rows, 128), BF16),
            dma((9,)),
            dma((4,)),
            pltpu.VMEM((2, plane, width), BF16),
            pltpu.VMEM((wide, width), BF16),
            pltpu.VMEM((wide, width), BF16),
            pltpu.VMEM((count, width), BF16),
            pltpu.VMEM((count, cols), BF16),
            pltpu.VMEM((wide // BLK, BLK, 2 * cols), BF16),
            pltpu.VMEM((count, cols), BF16),
            pltpu.VMEM((count, cols), BF16),
            pltpu.VMEM((wide, 2 * cols), F32),
            pltpu.VMEM((blocks, BLK, 2 * cols), F32),
            pltpu.VMEM((count, cols), BF16),
            pltpu.VMEM((wide, 2 * cols), BF16),
            pltpu.VMEM((2, plane, 2 * cols), BF16),
            pltpu.VMEM((count, width), F32),
            pltpu.VMEM((count, width), BF16),
            pltpu.VMEM((count, width), BF16),
            pltpu.VMEM((count, width), F32),
            pltpu.VMEM((count, width), F32),
            pltpu.VMEM((count, width), BF16),
            pltpu.VMEM((count, width), BF16),
            pltpu.VMEM((2 * plane, width), BF16),
            pltpu.VMEM((2 * plane, width), BF16),
            pltpu.VMEM((rows, 128), F32),
            pltpu.VMEM((2, rows // 2, 128), BF16),
            pltpu.VMEM((2, rows // 2, 128), BF16),
            pltpu.VMEM((tap_links, 8, width), F32),
            pltpu.VMEM((len(tap_radix) + 1, 8, width), F32),
        ]
        + [dma(shape) for shape in semaphores for _ in range(2)],
        compiler_params=pltpu.CompilerParams(
            collective_id=0, has_side_effects=True, vmem_limit_bytes=60 * MIB
        ),
    )(
        key_blocks.T,
        counts,
        tokens,
        cotangent,
        stem_taps,
        query_weight,
        key_weight,
        value_weight,
        out_weight,
    )
    weight = sds((depth, cols), F32)
    out_grad = sds((cols, depth), F32)
    gqw, gkw, gvw, go, grad_taps, layer_out, grad_tokens = pl.pallas_call(
        unpack_kernel,
        out_shape=[
            weight,
            weight,
            weight,
            out_grad,
            sds(stem_taps.shape, F32),
            sds((count, width), BF16),
            sds((count, width), F32),
        ],
        in_specs=[HBM] * 4,
        out_specs=[HBM] * 7,
        scratch_shapes=[pltpu.VMEM(final.shape, BF16)]
        + [pltpu.VMEM(shape.shape, F32) for shape in (weight, weight, weight, out_grad)]
        + [dma((4,)), dma((7,))],
        compiler_params=pltpu.CompilerParams(vmem_limit_bytes=60 * MIB),
    )(final, taps, layer_out, grad_tokens)
    return (layer_out, grad_tokens, grad_taps, gqw, gkw, gvw, go)


def solution(mesh):
    in_specs = (
        P("slab", "tp"),
        P(None, "tp"),
        P(None, "tp"),
        P(None, "tp"),
        P(None, "tp"),
        P("tp", None),
        P("slab", None),
        P("slab"),
        P("slab", "tp"),
    )
    out_specs = (
        P("slab", "tp"),
        P("slab", "tp"),
        P(None, "tp"),
        P(None, "tp"),
        P(None, "tp"),
        P(None, "tp"),
        P("tp", None),
    )
    return jax.shard_map(
        functools.partial(body, mesh.shape["slab"]),
        mesh=mesh,
        in_specs=in_specs,
        out_specs=out_specs,
        check_vma=False,
    )
```

```python
import functools

import jax
import jax.numpy as jnp
from jax import lax
from jax.experimental import pallas as pl
from jax.experimental.pallas import tpu as pltpu
from jax.sharding import PartitionSpec as P

HD = 64
BLK = 128
PLANE_TOK = 512
MAXK = 4
NEG = -1e30
F32 = jnp.float32
BF16 = jnp.bfloat16
MESH = pl.DeviceIdType.MESH
HBM = pl.BlockSpec(memory_space=pltpu.HBM)
MIB = 1024 * 1024
CHUNK = 256


def mm(a, b):
    return jnp.dot(a, b, preferred_element_type=F32)


def mm_nt(a, b):
    return lax.dot_general(a, b, (((1,), (1,)), ((), ())), preferred_element_type=F32)


def mm_tn(a, b):
    return lax.dot_general(a, b, (((0,), (0,)), ((), ())), preferred_element_type=F32)


def part(index, width):
    return pl.ds(pl.multiple_of(index * width, width), width)


def copy_to(src, dst, send, recv, where):
    return pltpu.make_async_remote_copy(
        src_ref=src,
        dst_ref=dst,
        send_sem=send,
        recv_sem=recv,
        device_id=where,
        device_id_type=MESH,
    )


def layer_kernel(
    slabs,
    blocks_in,
    counts_in,
    tok_in,
    cot_in,
    taps_in_ref,
    wq_in,
    wk_in,
    wv_in,
    ow_in,
    layer_out_ref,
    grad_out_ref,
    final_out_ref,
    taps_out_ref,
    blocks_ref,
    counts_ref,
    tok_ref,
    cot_ref,
    taps_ref,
    wq_ref,
    wk_ref,
    wv_ref,
    ow_ref,
    layer_ref,
    grad_ref,
    final,
    load_sem,
    store_sem,
    halo,
    so,
    st,
    ct,
    q,
    kv,
    grad,
    attn,
    acc,
    spare,
    held,
    gq_all,
    low,
    from_halo,
    mix,
    mix_out,
    mix_in,
    own,
    other,
    part_out,
    part_in,
    edge,
    edge_in,
    wsum,
    outgoing,
    incoming,
    taps_in,
    taps_sum,
    t_send,
    t_recv,
    s_send,
    s_recv,
    c_send,
    c_recv,
    so_send,
    so_recv,
    st_send,
    st_recv,
    h_send,
    h_recv,
    m_send,
    m_recv,
    p_send,
    p_recv,
    e_send,
    e_recv,
    w_send,
    w_recv,
    g_send,
    g_recv,
):
    me = lax.axis_index("slab")
    tp = lax.axis_index("tp")
    core = lax.rem(me, 2)
    count_bits = slabs.bit_length() - 1
    groups = [(0, 1), (1, 1)] + [(b, min(2, count_bits - b)) for b in range(2, count_bits, 2)]
    tap_groups = [(0, 1)] + [(b, min(3, count_bits - b)) for b in range(1, count_bits, 3)]
    stages = len(groups)
    tokens, width = tok_ref.shape
    cols, depth = ow_ref.shape
    heads = cols // HD
    planes = tokens // PLANE_TOK
    total = planes * slabs
    per_plane = PLANE_TOK // BLK
    pieces = PLANE_TOK // CHUNK
    halves = cols // 128
    last = planes - 1
    span = wsum.shape[0] // 2
    mine, theirs = part(tp, width), part(1 - tp, width)
    mate = {"tp": 1 - tp}
    slow = {"slab": lax.rem(me + slabs + 2 * core - 1, slabs)}
    fast = {"slab": me + 1 - 2 * core}
    sides = (slow, fast)
    sent = []

    def bit_of(b):
        return lax.rem(lax.div(me, 1 << b), 2)

    def digit_of(group, flip):
        first, size = group
        total_of = 0
        for n in range(size):
            bit = bit_of(first + n)
            total_of = total_of + ((1 - bit) if flip >> n & 1 else bit) * (1 << n)
        return total_of

    def peer_at(flip):
        move = 0
        for b in range(count_bits):
            if flip >> b & 1:
                move = move + (1 - 2 * bit_of(b)) * (1 << b)
        return {"slab": me + move}

    def peer(group, flip):
        return peer_at(flip << group[0])

    def peers(group):
        return [peer(group, flip) for flip in range(1, 1 << group[1])]

    def plane_of(k):
        return core * last + (1 - 2 * core) * k

    def nat(k, c, size=CHUNK):
        return pl.ds(pl.multiple_of(plane_of(k) * PLANE_TOK + c * size, size), size)

    def loc(k, c, size=CHUNK):
        return pl.ds(k * PLANE_TOK + c * size, size)

    barrier = pltpu.get_barrier_semaphore()
    flips = {
        flip << group[0] for group in groups + tap_groups for flip in range(1, 1 << group[1])
    }
    greeted = [slow, mate] + [peer_at(flip) for flip in sorted(flips)]
    for where in greeted:
        pl.semaphore_signal(barrier, inc=1, device_id=where, device_id_type=MESH)
    loads = {}
    for n, (name, src, dst) in enumerate(
        (
            ("tokens", tok_in, tok_ref),
            ("taps", taps_in_ref, taps_ref),
            ("key", wk_in, wk_ref),
            ("value", wv_in, wv_ref),
            ("query", wq_in, wq_ref),
            ("out", ow_in, ow_ref),
            ("cot", cot_in, cot_ref),
            ("blocks", blocks_in, blocks_ref),
            ("counts", counts_in, counts_ref),
        )
    ):
        loads[name] = pltpu.make_async_copy(src, dst, load_sem.at[n])
        loads[name].start()
    pl.semaphore_wait(barrier, len(greeted))

    def launch(copy):
        copy.start()
        sent.append(copy)
        return copy

    halos = {}
    for c in range(pieces):
        for side, k in ((0, 0), (1, last)):
            halos[side, c] = launch(
                copy_to(
                    tok_in.at[nat(k, c)], halo.at[side, loc(0, c)],
                    t_send.at[side, c], t_recv.at[side, c], sides[side],
                )
            )
    cots = {
        (k, c): copy_to(
            cot_in.at[nat(k, c)], ct.at[nat(k, c)],
            c_send.at[k * pieces + c], c_recv.at[k * pieces + c], mate,
        )
        for k in range(planes)
        for c in range(pieces)
    }
    waiting = list(cots)
    launch(cots[waiting.pop(0)])

    loads["tokens"].wait()
    loads["taps"].wait()
    tap_low = taps_ref[pl.ds(2 * core, 1), :]
    tap_mid = taps_ref[1:2, :]
    tap_high = taps_ref[pl.ds(2 - 2 * core, 1), :]

    def tokens_at(k, c):
        if k < 0:
            return halo[0, loc(0, c), :].astype(F32)
        if k > last:
            return halo[1, loc(0, c), :].astype(F32)
        return tok_ref[nat(k, c), :].astype(F32)

    def edges_of(k):
        return [(0, 0)] * (k == 0) + [(1, planes + 1)] * (k == last)

    order = [(k, c) for k in reversed(range(planes)) for c in range(pieces)]
    stems, so_halo, st_halo = {}, {}, {}
    for k, c in order:
        for side, _ in edges_of(k):
            halos[side, c].wait_recv()
        rows = loc(k + 1, c)
        so[rows, :] = (
            tap_low * tokens_at(k - 1, c) + tap_mid * tokens_at(k, c) + tap_high * tokens_at(k + 1, c)
        ).astype(BF16)
        stems[k, c] = launch(
            copy_to(
                so.at[rows], st.at[rows], s_send.at[k * pieces + c], s_recv.at[k * pieces + c], mate
            )
        )
        for side, e in edges_of(k):
            so_halo[side, c] = launch(
                copy_to(
                    so.at[rows], so.at[loc(e, c)],
                    so_send.at[side, c], so_recv.at[side, c], sides[side],
                )
            )

    def project(w_ref, rows):
        return (mm(so[rows, :], w_ref[mine, :]) + mm(st[rows, :], w_ref[theirs, :])).astype(BF16)

    def keys_values(rows):
        for half, w_ref in enumerate((wk_ref, wv_ref)):
            value = project(w_ref, rows)
            for n in range(CHUNK // BLK):
                kv[rows.start // BLK + n, :, half * cols : (half + 1) * cols] = value[
                    n * BLK : (n + 1) * BLK
                ]

    for name in ("key", "value", "query", "out", "cot", "blocks", "counts"):
        loads[name].wait()
    for n, (k, c) in enumerate(order):
        rows = loc(k + 1, c)
        stems[k, c].wait_recv()
        for side, e in edges_of(k):
            st_halo[side, c] = launch(
                copy_to(
                    st.at[rows], st.at[loc(e, c)],
                    st_send.at[side, c], st_recv.at[side, c], sides[side],
                )
            )
        if n == len(order) - 2:
            launch(cots[waiting.pop(0)])
        if n == len(order) - 1:
            for name in waiting:
                launch(cots[name])
        keys_values(rows)
        q[nat(k, c), :] = project(wq_ref, rows)

    def output_gradient(k):
        for c in range(pieces):
            rows = nat(k, c)
            cots[k, c].wait_recv()
            grad[rows, :] = (
                mm_nt(cot_ref[rows, :], ow_ref[:, mine]) + mm_nt(ct[rows, :], ow_ref[:, theirs])
            ).astype(BF16)

    def halo_keys(side, e):
        for c in range(pieces):
            so_halo[side, c].wait_recv()
            st_halo[side, c].wait_recv()
            keys_values(loc(e, c))

    lane = lax.broadcasted_iota(jnp.int32, (1, cols), 1) // HD
    masks = [(lane == h).astype(F32).astype(BF16) for h in range(heads)]

    def stack(block):
        return jnp.concatenate([block * mask for mask in masks], axis=0)

    def pick(value):
        heads_t = [
            value[h * HD : (h + 1) * HD, h * BLK : (h + 1) * BLK] for h in range(heads)
        ]
        return jnp.concatenate(heads_t, axis=0).T

    def free_slot(k, j):
        block = blocks_ref[MAXK - 1, plane_of(k) * per_plane + j]
        plane = lax.rem(
            lax.div(block, per_plane) - me * planes - plane_of(k) + 1 + total, total
        )
        plane = k + core * 2 + (1 - 2 * core) * jnp.minimum(plane, 2)
        return plane * per_plane + lax.rem(block, per_plane)

    fixed = (MAXK - 1) * BLK

    def block_inputs(k, j):
        where = [e * per_plane + j for e in range(k, k + 3)] + [free_slot(k, j)]
        pairs = [kv[at] for at in where]
        keys = jnp.concatenate([pair[:, :cols] for pair in pairs], axis=0)
        values = jnp.concatenate([pair[:, cols:] for pair in pairs], axis=0)
        queries = stack(q[nat(k, j, BLK), :] * jnp.asarray(HD**-0.5, BF16))
        return keys, values, queries

    def attention_forward(k):
        for j in range(per_plane):
            keys, values, queries = block_inputs(k, j)
            scores = mm_nt(keys, queries)
            left_out = MAXK - counts_ref[plane_of(k) * per_plane + j]
            scores = jnp.concatenate(
                [scores[:fixed], scores[fixed:] + left_out.astype(F32) * NEG], axis=0
            )
            exps = jnp.exp(scores - jnp.max(scores, axis=0, keepdims=True))
            probs = exps * (1.0 / jnp.sum(exps, axis=0, keepdims=True))
            held[k * per_plane + j] = probs
            attn[nat(k, j, BLK), :] = pick(mm_tn(values, probs.astype(BF16))).astype(BF16)

    def attention_backward(k):
        for j in range(per_plane):
            keys, values, queries = block_inputs(k, j)
            grads = stack(grad[nat(k, j, BLK), :])
            probs = held[k * per_plane + j]
            gprobs = mm_nt(values, grads)
            inner = jnp.sum(probs * gprobs, axis=0, keepdims=True)
            gscores = (probs * (gprobs - inner)).astype(BF16)
            gq_all[loc(k, j, BLK), :] = (pick(mm_tn(keys, gscores)) * (HD**-0.5)).astype(BF16)
            gkeys = mm(gscores, queries)
            gvalues = mm(probs.astype(BF16), grads)
            for half, g in enumerate((gkeys, gvalues)):
                columns = slice(half * cols, (half + 1) * cols)
                for n in range(3):
                    place = loc(k + n, j, BLK)
                    if k == 0 or n == 2:
                        acc[place, columns] = g[n * BLK : (n + 1) * BLK]
                    else:
                        acc[place, columns] += g[n * BLK : (n + 1) * BLK]
                spare[k * per_plane + j, :, columns] = g[fixed:]

    def collect(e):
        @pl.loop(0, per_plane)
        def _(t):
            at = pl.ds(pl.multiple_of(e * PLANE_TOK + t * BLK, BLK), BLK)
            value = acc[at, :]
            for k in range(max(e - 2, 0), min(e, last) + 1):
                for step in range(1, per_plane):
                    j = lax.rem(t + step, per_plane)
                    off = free_slot(k, j) - (e * per_plane + t)
                    hit = (1 - jnp.minimum(off * off, 1)).astype(F32)
                    value = value + hit * spare[k * per_plane + j]
            if 1 <= e <= planes:
                acc[at, :] = value
            low[at, :] = value.astype(BF16)

    returns = {}

    def give_back(side, e):
        rows = loc(e, 0, PLANE_TOK)
        returns[side] = launch(
            copy_to(
                low.at[rows], from_halo.at[side], h_send.at[side], h_recv.at[side], sides[side]
            )
        )

    mixes = {}

    def mix_heads(k):
        rows = nat(k, 0, PLANE_TOK)
        mix_out[rows, :] = mm(attn[rows, :], ow_ref[:, theirs]).astype(BF16)
        mixes[k] = launch(
            copy_to(mix_out.at[rows], mix_in.at[rows], m_send.at[k], m_recv.at[k], mate)
        )
        mix[rows, :] = mm(attn[rows, :], ow_ref[:, mine])

    halo_keys(1, planes + 1)
    for k in reversed(range(planes)):
        if k == 0:
            halo_keys(0, 0)
        attention_forward(k)
        if k > 0:
            mix_heads(k)
    for k in range(planes):
        output_gradient(k)
        attention_backward(k)
        if k == 0:
            collect(0)
            give_back(0, 0)
            mix_heads(0)
        if k == last:
            collect(planes + 1)
            give_back(1, planes + 1)

    orders = (groups[:1] + groups[2:] + groups[1:2], groups)
    sizes = []
    for order_of in orders:
        left = [span]
        for _, size in order_of:
            left.append(left[-1] >> size)
        sizes.append(left)
    lows = [jnp.int32(0), jnp.int32(span)]
    trail = [[], []]
    step_of = [0, 0]
    flight = [[], []]
    links = [0, 0]

    def rows_at(at, size):
        return pl.ds(pl.multiple_of(at, 16), size)

    def travel(t, src, dst, where):
        n = links[t]
        links[t] = n + 1
        flight[t].append(launch(copy_to(src, dst, w_send.at[t, n], w_recv.at[t, n], where)))

    def slot_of(t, k, flip):
        size = sizes[t][k + 1]
        return pl.ds(span - sizes[t][k] + (flip - 1) * size, size)

    def advance(t):
        k = step_of[t]
        if k > 2 * stages:
            return
        for copy in flight[t]:
            copy.wait_recv()
        flight[t] = []
        if 1 <= k <= stages:
            at = rows_at(lows[t], sizes[t][k])
            value = wsum[at, :]
            for flip in range(1, 1 << orders[t][k - 1][1]):
                value = value + incoming[t, slot_of(t, k - 1, flip), :].astype(F32)
            if k < stages:
                wsum[at, :] = value
            else:
                final[at, :] = value.astype(BF16)
        if k < stages:
            group, size = orders[t][k], sizes[t][k + 1]
            for flip in range(1, 1 << group[1]):
                slots = slot_of(t, k, flip)
                give = lows[t] + digit_of(group, flip) * size
                outgoing[t, slots, :] = wsum[rows_at(give, size), :].astype(BF16)
                travel(t, outgoing.at[t, slots], incoming.at[t, slots], peer(group, flip))
            lows[t] = lows[t] + digit_of(group, 0) * size
            trail[t].append(lows[t])
        elif k < 2 * stages:
            j = 2 * stages - 1 - k
            at = rows_at(trail[t][j], sizes[t][j + 1])
            for where in peers(orders[t][j]):
                travel(t, final.at[at], final.at[at], where)
        step_of[t] = k + 1

    def weight_gradient(base, rows, g):
        for index, s_ref in ((tp, so), (1 - tp, st)):
            product = mm_tn(s_ref[rows, :], g)
            for half in range(halves):
                at = pl.multiple_of(base + half * depth + index * width, 128)
                wsum[pl.ds(at, width), :] = product[:, half * 128 : (half + 1) * 128]

    block = depth * halves
    inside = slice(PLANE_TOK, PLANE_TOK + tokens)
    weight_gradient(0, inside, gq_all[...])
    for index, c_ref in ((tp, cot_ref), (1 - tp, ct)):
        product = mm_tn(attn[...], c_ref[...])
        for half in range(width // 128):
            wsum[pl.ds(pl.multiple_of(block + (index * (width // 128) + half) * cols, 128), cols), :] = (
                product[:, half * 128 : (half + 1) * 128]
            )
    advance(0)
    for e in range(1, planes + 1):
        collect(e)
    everything = slice(0, low.shape[0])
    weight_gradient(2 * block, everything, low[:, :cols])
    weight_gradient(3 * block, everything, low[:, cols:])
    advance(1)
    advance(0)
    for k in range(planes):
        for c in range(pieces):
            rows = loc(k, c)
            gq = gq_all[rows, :]
            own[rows, :] = mm_nt(gq, wq_ref[mine, :])
            other[rows, :] = mm_nt(gq, wq_ref[theirs, :])
    advance(1)
    parts = {}
    stores = []

    def mix_add():
        for k in reversed(range(planes)):
            rows = nat(k, 0, PLANE_TOK)
            mixes[k].wait_recv()
            layer_ref[rows, :] = (
                so[loc(k + 1, 0, PLANE_TOK), :].astype(F32)
                + (mix[rows, :] + mix_in[rows, :].astype(F32))
            ).astype(BF16)
        stores.append(pltpu.make_async_copy(layer_ref, layer_out_ref, store_sem.at[0]))
        stores[-1].start()

    for k in reversed(range(planes)):
        for side, _ in edges_of(k):
            returns[side].wait_recv()
        for c in range(pieces):
            rows = loc(k, c)
            value = acc[loc(k + 1, c), :]
            for side, _ in edges_of(k):
                value = value + from_halo[side, loc(0, c), :].astype(F32)
            value = value.astype(BF16)
            gk, gv = value[:, :cols], value[:, cols:]
            part_out[rows, :] = (
                other[rows, :] + mm_nt(gk, wk_ref[theirs, :]) + mm_nt(gv, wv_ref[theirs, :])
            ).astype(BF16)
            parts[k, c] = launch(
                copy_to(
                    part_out.at[rows], part_in.at[rows],
                    p_send.at[k * pieces + c], p_recv.at[k * pieces + c], mate,
                )
            )
            own[rows, :] += mm_nt(gk, wk_ref[mine, :]) + mm_nt(gv, wv_ref[mine, :])
        if k == last:
            mix_add()
    advance(1)
    edges = {}
    sums = [jnp.zeros((1, width), F32) for _ in range(3)]
    turns = [(), (0,), (0, 1), ()]
    for k in reversed(range(planes)):
        for c in range(pieces):
            rows = loc(k, c)
            parts[k, c].wait_recv()
            stem_grad = cot_ref[nat(k, c), :].astype(F32) + (
                own[rows, :] + part_in[rows, :].astype(F32)
            )
            own[rows, :] = stem_grad
            for side, _ in edges_of(k):
                at = loc(side, c)
                edge[at, :] = stem_grad.astype(BF16)
                edges[side, c] = launch(
                    copy_to(
                        edge.at[at], edge_in.at[at],
                        e_send.at[side, c], e_recv.at[side, c], sides[side],
                    )
                )
            for n in range(3):
                sums[n] = sums[n] + jnp.sum(
                    stem_grad * tokens_at(k - 1 + n, c), axis=0, keepdims=True
                )
            for t in turns.pop(0) if turns else ():
                advance(t)
    swap = core == 1
    sums = [jnp.where(swap, sums[2], sums[0]), sums[1], jnp.where(swap, sums[0], sums[2])]
    taps_sum[0] = jnp.concatenate(sums + [jnp.zeros((5, width), F32)], axis=0)

    def send_taps(k):
        base = sum((1 << size) - 1 for _, size in tap_groups[:k])
        return [
            launch(
                copy_to(
                    taps_sum.at[k], taps_in.at[base + n],
                    g_send.at[base + n], g_recv.at[base + n], where,
                )
            )
            for n, where in enumerate(peers(tap_groups[k]))
        ]

    def take_taps(k, copies):
        base = sum((1 << size) - 1 for _, size in tap_groups[:k])
        value = taps_sum[k]
        for n, copy in enumerate(copies):
            copy.wait_recv()
            value = value + taps_in[base + n]
        taps_sum[k + 1] = value

    def gradient_at(k, c):
        if k < 0:
            return edge_in[loc(0, c), :].astype(F32)
        if k > last:
            return edge_in[loc(1, c), :].astype(F32)
        return own[loc(k, c), :]

    def finish_tokens():
        for copy in edges.values():
            copy.wait_recv()
        for k in range(planes):
            for c in range(pieces):
                grad_ref[nat(k, c), :] = (
                    tap_low * gradient_at(k + 1, c) + tap_mid * gradient_at(k, c)
                    + tap_high * gradient_at(k - 1, c)
                )
        stores.append(pltpu.make_async_copy(grad_ref, grad_out_ref, store_sem.at[1]))
        stores[-1].start()

    for k in range(len(tap_groups)):
        copies = send_taps(k)
        advance(0)
        advance(1)
        if k == 0:
            finish_tokens()
        take_taps(k, copies)
    for _ in range(2 * stages):
        advance(0)
        advance(1)
    stores.append(pltpu.make_async_copy(final, final_out_ref, store_sem.at[2]))
    stores.append(
        pltpu.make_async_copy(taps_sum.at[len(tap_groups)], taps_out_ref, store_sem.at[3])
    )
    for store in stores[-2:]:
        store.start()
    for store in stores:
        store.wait()
    for copy in sent:
        copy.wait_send()


def unpack_kernel(
    final_in, taps_in, layer_in, grad_in, gqw_ref, gkw_ref, gvw_ref, go_ref, taps_ref,
    layer_ref, grad_ref, final, taps, layer, grad, gqw, gkw, gvw, go, load_sem, sem,
):
    outs = ((gqw, gqw_ref), (go, go_ref), (gkw, gkw_ref), (gvw, gvw_ref))
    part_rows = final.shape[0] // len(outs)
    pieces = [pl.ds(n * part_rows, part_rows) for n in range(len(outs))]
    moves = [(final_in.at[at], final.at[at]) for at in pieces]
    moves += [(taps_in, taps), (layer_in, layer)]
    halves = [pl.ds(n * (grad.shape[0] // 2), grad.shape[0] // 2) for n in range(2)]
    moves += [(grad_in.at[at], grad.at[at]) for at in halves]
    loads = [
        pltpu.make_async_copy(a, b, load_sem.at[n]) for n, (a, b) in enumerate(moves)
    ]
    for load in loads:
        load.start()
    stores = []

    def store(a, b):
        stores.append(pltpu.make_async_copy(a, b, sem.at[len(stores)]))
        stores[-1].start()

    at = 0
    for n, (out, dst) in enumerate(outs):
        loads[n].wait()
        rows = out.shape[0]
        for half in range(out.shape[1] // 128):
            out[:, half * 128 : (half + 1) * 128] = final[at : at + rows, :].astype(F32)
            at += rows
        store(out, dst)
    loads[4].wait()
    store(taps.at[0 : taps_ref.shape[0]], taps_ref)
    loads[5].wait()
    store(layer, layer_ref)
    for n, at in enumerate(halves):
        loads[6 + n].wait()
        store(grad.at[at], grad_ref.at[at])
    for copy in stores:
        copy.wait()


def body(
    slabs,
    tokens,
    stem_taps,
    query_weight,
    key_weight,
    value_weight,
    out_weight,
    key_blocks,
    counts,
    cotangent,
):
    count, width = tokens.shape
    depth, cols = query_weight.shape
    plane = PLANE_TOK
    planes = count // plane
    sds = jax.ShapeDtypeStruct
    count_bits = slabs.bit_length() - 1
    radix = [2, 2] + [1 << min(2, count_bits - b) for b in range(2, count_bits, 2)]
    links = sum(radix) - len(radix)
    tap_radix = [2] + [1 << min(3, count_bits - b) for b in range(1, count_bits, 3)]
    tap_links = sum(tap_radix) - len(tap_radix)
    chunks = count // CHUNK
    pieces = plane // CHUNK
    blocks = count // BLK
    wide = count + 2 * plane
    dma = pltpu.SemaphoreType.DMA
    rows = 4 * depth * cols // 128
    semaphores = [
        (2, pieces),
        (chunks,),
        (chunks,),
        (2, pieces),
        (2, pieces),
        (2,),
        (planes,),
        (chunks,),
        (2, pieces),
        (2, 2 * links),
        (tap_links,),
    ]
    layer_out, grad_tokens, final, taps = pl.pallas_call(
        functools.partial(layer_kernel, slabs),
        out_shape=[
            sds((count, width), BF16),
            sds((count, width), F32),
            sds((rows, 128), BF16),
            sds((8, width), F32),
        ],
        in_specs=[HBM] * 9,
        out_specs=[HBM] * 4,
        scratch_shapes=[
            pltpu.SMEM((MAXK, blocks), jnp.int32),
            pltpu.SMEM((blocks,), jnp.int32),
            pltpu.VMEM((count, width), BF16),
            pltpu.VMEM((count, width), BF16),
            pltpu.VMEM(stem_taps.shape, F32),
            pltpu.VMEM((depth, cols), BF16),
            pltpu.VMEM((depth, cols), BF16),
            pltpu.VMEM((depth, cols), BF16),
            pltpu.VMEM((cols, depth), BF16),
            pltpu.VMEM((count, width), BF16),
            pltpu.VMEM((count, width), F32),
            pltpu.VMEM((rows, 128), BF16),
            dma((9,)),
            dma((4,)),
            pltpu.VMEM((2, plane, width), BF16),
            pltpu.VMEM((wide, width), BF16),
            pltpu.VMEM((wide, width), BF16),
            pltpu.VMEM((count, width), BF16),
            pltpu.VMEM((count, cols), BF16),
            pltpu.VMEM((wide // BLK, BLK, 2 * cols), BF16),
            pltpu.VMEM((count, cols), BF16),
            pltpu.VMEM((count, cols), BF16),
            pltpu.VMEM((wide, 2 * cols), F32),
            pltpu.VMEM((blocks, BLK, 2 * cols), F32),
            pltpu.VMEM((blocks, MAXK * BLK, cols // HD * BLK), F32),
            pltpu.VMEM((count, cols), BF16),
            pltpu.VMEM((wide, 2 * cols), BF16),
            pltpu.VMEM((2, plane, 2 * cols), BF16),
            pltpu.VMEM((count, width), F32),
            pltpu.VMEM((count, width), BF16),
            pltpu.VMEM((count, width), BF16),
            pltpu.VMEM((count, width), F32),
            pltpu.VMEM((count, width), F32),
            pltpu.VMEM((count, width), BF16),
            pltpu.VMEM((count, width), BF16),
            pltpu.VMEM((2 * plane, width), BF16),
            pltpu.VMEM((2 * plane, width), BF16),
            pltpu.VMEM((rows, 128), F32),
            pltpu.VMEM((2, rows // 2, 128), BF16),
            pltpu.VMEM((2, rows // 2, 128), BF16),
            pltpu.VMEM((tap_links, 8, width), F32),
            pltpu.VMEM((len(tap_radix) + 1, 8, width), F32),
        ]
        + [dma(shape) for shape in semaphores for _ in range(2)],
        compiler_params=pltpu.CompilerParams(
            collective_id=0, has_side_effects=True, vmem_limit_bytes=60 * MIB
        ),
    )(
        key_blocks.T,
        counts,
        tokens,
        cotangent,
        stem_taps,
        query_weight,
        key_weight,
        value_weight,
        out_weight,
    )
    weight = sds((depth, cols), F32)
    out_grad = sds((cols, depth), F32)
    gqw, gkw, gvw, go, grad_taps, layer_out, grad_tokens = pl.pallas_call(
        unpack_kernel,
        out_shape=[
            weight,
            weight,
            weight,
            out_grad,
            sds(stem_taps.shape, F32),
            sds((count, width), BF16),
            sds((count, width), F32),
        ],
        in_specs=[HBM] * 4,
        out_specs=[HBM] * 7,
        scratch_shapes=[
            pltpu.VMEM(x.shape, x.dtype)
            for x in (final, taps, layer_out, grad_tokens, weight, weight, weight, out_grad)
        ]
        + [dma((8,)), dma((8,))],
        compiler_params=pltpu.CompilerParams(vmem_limit_bytes=60 * MIB),
    )(final, taps, layer_out, grad_tokens)
    return (layer_out, grad_tokens, grad_taps, gqw, gkw, gvw, go)


def solution(mesh):
    in_specs = (
        P("slab", "tp"),
        P(None, "tp"),
        P(None, "tp"),
        P(None, "tp"),
        P(None, "tp"),
        P("tp", None),
        P("slab", None),
        P("slab"),
        P("slab", "tp"),
    )
    out_specs = (
        P("slab", "tp"),
        P("slab", "tp"),
        P(None, "tp"),
        P(None, "tp"),
        P(None, "tp"),
        P(None, "tp"),
        P("tp", None),
    )
    return jax.shard_map(
        functools.partial(body, mesh.shape["slab"]),
        mesh=mesh,
        in_specs=in_specs,
        out_specs=out_specs,
        check_vma=False,
    )
```

```python
import functools

import jax
import jax.numpy as jnp
from jax import lax
from jax.experimental import pallas as pl
from jax.experimental.pallas import tpu as pltpu
from jax.sharding import PartitionSpec as P

HD = 64
BLK = 128
PLANE_TOK = 512
MAXK = 4
NEG = -1e30
F32 = jnp.float32
BF16 = jnp.bfloat16
MESH = pl.DeviceIdType.MESH
HBM = pl.BlockSpec(memory_space=pltpu.HBM)
MIB = 1024 * 1024
CHUNK = 256


def mm(a, b):
    return jnp.dot(a, b, preferred_element_type=F32)


def mm_nt(a, b):
    return lax.dot_general(a, b, (((1,), (1,)), ((), ())), preferred_element_type=F32)


def mm_tn(a, b):
    return lax.dot_general(a, b, (((0,), (0,)), ((), ())), preferred_element_type=F32)


def part(index, width):
    return pl.ds(pl.multiple_of(index * width, width), width)


def copy_to(src, dst, send, recv, where):
    return pltpu.make_async_remote_copy(
        src_ref=src,
        dst_ref=dst,
        send_sem=send,
        recv_sem=recv,
        device_id=where,
        device_id_type=MESH,
    )


def layer_kernel(
    slabs,
    blocks_in,
    counts_in,
    tok_in,
    cot_in,
    taps_in_ref,
    wq_in,
    wk_in,
    wv_in,
    ow_in,
    layer_out_ref,
    grad_out_ref,
    final_out_ref,
    taps_out_ref,
    blocks_ref,
    counts_ref,
    tok_ref,
    cot_ref,
    taps_ref,
    wq_ref,
    wk_ref,
    wv_ref,
    ow_ref,
    layer_ref,
    grad_ref,
    final,
    load_sem,
    store_sem,
    halo,
    so,
    st,
    ct,
    q,
    kv,
    grad,
    attn,
    acc,
    spare,
    held,
    gq_all,
    low,
    from_halo,
    mix,
    mix_out,
    mix_in,
    own,
    other,
    part_out,
    part_in,
    edge,
    edge_in,
    wsum,
    outgoing,
    incoming,
    taps_in,
    taps_sum,
    t_send,
    t_recv,
    s_send,
    s_recv,
    c_send,
    c_recv,
    so_send,
    so_recv,
    st_send,
    st_recv,
    h_send,
    h_recv,
    m_send,
    m_recv,
    p_send,
    p_recv,
    e_send,
    e_recv,
    w_send,
    w_recv,
    g_send,
    g_recv,
):
    me = lax.axis_index("slab")
    tp = lax.axis_index("tp")
    core = lax.rem(me, 2)
    count_bits = slabs.bit_length() - 1
    groups = [(0, 1), (1, 1)] + [(b, min(2, count_bits - b)) for b in range(2, count_bits, 2)]
    tap_groups = [(0, 1)] + [(b, min(3, count_bits - b)) for b in range(1, count_bits, 3)]
    stages = len(groups)
    tokens, width = tok_ref.shape
    cols, depth = ow_ref.shape
    heads = cols // HD
    planes = tokens // PLANE_TOK
    total = planes * slabs
    per_plane = PLANE_TOK // BLK
    pieces = PLANE_TOK // CHUNK
    halves = cols // 128
    last = planes - 1
    span = wsum.shape[0] // 2
    mine, theirs = part(tp, width), part(1 - tp, width)
    mate = {"tp": 1 - tp}
    slow = {"slab": lax.rem(me + slabs + 2 * core - 1, slabs)}
    fast = {"slab": me + 1 - 2 * core}
    sides = (slow, fast)
    sent = []

    def bit_of(b):
        return lax.rem(lax.div(me, 1 << b), 2)

    def digit_of(group, flip):
        first, size = group
        total_of = 0
        for n in range(size):
            bit = bit_of(first + n)
            total_of = total_of + ((1 - bit) if flip >> n & 1 else bit) * (1 << n)
        return total_of

    def peer_at(flip):
        move = 0
        for b in range(count_bits):
            if flip >> b & 1:
                move = move + (1 - 2 * bit_of(b)) * (1 << b)
        return {"slab": me + move}

    def peer(group, flip):
        return peer_at(flip << group[0])

    def peers(group):
        return [peer(group, flip) for flip in range(1, 1 << group[1])]

    def plane_of(k):
        return core * last + (1 - 2 * core) * k

    def nat(k, c, size=CHUNK):
        return pl.ds(pl.multiple_of(plane_of(k) * PLANE_TOK + c * size, size), size)

    def loc(k, c, size=CHUNK):
        return pl.ds(k * PLANE_TOK + c * size, size)

    barrier = pltpu.get_barrier_semaphore()
    flips = {
        flip << group[0] for group in groups + tap_groups for flip in range(1, 1 << group[1])
    }
    greeted = [slow, mate] + [peer_at(flip) for flip in sorted(flips)]
    for where in greeted:
        pl.semaphore_signal(barrier, inc=1, device_id=where, device_id_type=MESH)
    loads = {}
    for n, (name, src, dst) in enumerate(
        (
            ("tokens", tok_in, tok_ref),
            ("taps", taps_in_ref, taps_ref),
            ("key", wk_in, wk_ref),
            ("value", wv_in, wv_ref),
            ("query", wq_in, wq_ref),
            ("out", ow_in, ow_ref),
            ("cot", cot_in, cot_ref),
            ("blocks", blocks_in, blocks_ref),
            ("counts", counts_in, counts_ref),
        )
    ):
        loads[name] = pltpu.make_async_copy(src, dst, load_sem.at[n])
        loads[name].start()
    pl.semaphore_wait(barrier, len(greeted))

    def launch(copy):
        copy.start()
        sent.append(copy)
        return copy

    halos = {}
    for c in range(pieces):
        for side, k in ((0, 0), (1, last)):
            halos[side, c] = launch(
                copy_to(
                    tok_in.at[nat(k, c)], halo.at[side, loc(0, c)],
                    t_send.at[side, c], t_recv.at[side, c], sides[side],
                )
            )
    cots = {
        (k, c): copy_to(
            cot_in.at[nat(k, c)], ct.at[nat(k, c)],
            c_send.at[k * pieces + c], c_recv.at[k * pieces + c], mate,
        )
        for k in range(planes)
        for c in range(pieces)
    }
    waiting = list(cots)
    launch(cots[waiting.pop(0)])

    loads["tokens"].wait()
    loads["taps"].wait()
    tap_low = taps_ref[pl.ds(2 * core, 1), :]
    tap_mid = taps_ref[1:2, :]
    tap_high = taps_ref[pl.ds(2 - 2 * core, 1), :]

    def tokens_at(k, c):
        if k < 0:
            return halo[0, loc(0, c), :].astype(F32)
        if k > last:
            return halo[1, loc(0, c), :].astype(F32)
        return tok_ref[nat(k, c), :].astype(F32)

    def edges_of(k):
        return [(0, 0)] * (k == 0) + [(1, planes + 1)] * (k == last)

    order = [(k, c) for k in reversed(range(planes)) for c in range(pieces)]
    stems, so_halo, st_halo = {}, {}, {}
    for k, c in order:
        for side, _ in edges_of(k):
            halos[side, c].wait_recv()
        rows = loc(k + 1, c)
        so[rows, :] = (
            tap_low * tokens_at(k - 1, c) + tap_mid * tokens_at(k, c) + tap_high * tokens_at(k + 1, c)
        ).astype(BF16)
        stems[k, c] = launch(
            copy_to(
                so.at[rows], st.at[rows], s_send.at[k * pieces + c], s_recv.at[k * pieces + c], mate
            )
        )
        for side, e in edges_of(k):
            so_halo[side, c] = launch(
                copy_to(
                    so.at[rows], so.at[loc(e, c)],
                    so_send.at[side, c], so_recv.at[side, c], sides[side],
                )
            )

    def project(w_ref, rows):
        return (mm(so[rows, :], w_ref[mine, :]) + mm(st[rows, :], w_ref[theirs, :])).astype(BF16)

    def keys_values(rows):
        for half, w_ref in enumerate((wk_ref, wv_ref)):
            value = project(w_ref, rows)
            for n in range(CHUNK // BLK):
                kv[rows.start // BLK + n, :, half * cols : (half + 1) * cols] = value[
                    n * BLK : (n + 1) * BLK
                ]

    for name in ("key", "value", "query", "out", "cot", "blocks", "counts"):
        loads[name].wait()
    for n, (k, c) in enumerate(order):
        rows = loc(k + 1, c)
        stems[k, c].wait_recv()
        for side, e in edges_of(k):
            st_halo[side, c] = launch(
                copy_to(
                    st.at[rows], st.at[loc(e, c)],
                    st_send.at[side, c], st_recv.at[side, c], sides[side],
                )
            )
        if n == len(order) - 2:
            launch(cots[waiting.pop(0)])
        if n == len(order) - 1:
            for name in waiting:
                launch(cots[name])
        keys_values(rows)
        q[nat(k, c), :] = project(wq_ref, rows)

    def output_gradient(k):
        for c in range(pieces):
            rows = nat(k, c)
            cots[k, c].wait_recv()
            grad[rows, :] = (
                mm_nt(cot_ref[rows, :], ow_ref[:, mine]) + mm_nt(ct[rows, :], ow_ref[:, theirs])
            ).astype(BF16)

    def halo_keys(side, e):
        for c in range(pieces):
            so_halo[side, c].wait_recv()
            st_halo[side, c].wait_recv()
            keys_values(loc(e, c))

    lane = lax.broadcasted_iota(jnp.int32, (1, cols), 1) // HD
    masks = [(lane == h).astype(F32).astype(BF16) for h in range(heads)]

    def stack(block):
        return jnp.concatenate([block * mask for mask in masks], axis=0)

    def pick(value):
        heads_t = [
            value[h * HD : (h + 1) * HD, h * BLK : (h + 1) * BLK] for h in range(heads)
        ]
        return jnp.concatenate(heads_t, axis=0).T

    def free_slot(k, j):
        block = blocks_ref[MAXK - 1, plane_of(k) * per_plane + j]
        plane = lax.rem(
            lax.div(block, per_plane) - me * planes - plane_of(k) + 1 + total, total
        )
        plane = k + core * 2 + (1 - 2 * core) * jnp.minimum(plane, 2)
        return plane * per_plane + lax.rem(block, per_plane)

    fixed = (MAXK - 1) * BLK

    def block_inputs(k, j):
        where = [e * per_plane + j for e in range(k, k + 3)] + [free_slot(k, j)]
        pairs = [kv[at] for at in where]
        keys = jnp.concatenate([pair[:, :cols] for pair in pairs], axis=0)
        values = jnp.concatenate([pair[:, cols:] for pair in pairs], axis=0)
        queries = stack(q[nat(k, j, BLK), :] * jnp.asarray(HD**-0.5, BF16))
        return keys, values, queries

    def attention_forward(k):
        for j in range(per_plane):
            keys, values, queries = block_inputs(k, j)
            scores = mm_nt(keys, queries)
            left_out = MAXK - counts_ref[plane_of(k) * per_plane + j]
            scores = jnp.concatenate(
                [scores[:fixed], scores[fixed:] + left_out.astype(F32) * NEG], axis=0
            )
            exps = jnp.exp(scores - jnp.max(scores, axis=0, keepdims=True))
            probs = exps * (1.0 / jnp.sum(exps, axis=0, keepdims=True))
            held[k * per_plane + j] = probs
            attn[nat(k, j, BLK), :] = pick(mm_tn(values, probs.astype(BF16))).astype(BF16)

    def attention_backward(k):
        for j in range(per_plane):
            keys, values, queries = block_inputs(k, j)
            grads = stack(grad[nat(k, j, BLK), :])
            probs = held[k * per_plane + j]
            gprobs = mm_nt(values, grads)
            inner = jnp.sum(probs * gprobs, axis=0, keepdims=True)
            gscores = (probs * (gprobs - inner)).astype(BF16)
            gq_all[loc(k, j, BLK), :] = (pick(mm_tn(keys, gscores)) * (HD**-0.5)).astype(BF16)
            gkeys = mm(gscores, queries)
            gvalues = mm(probs.astype(BF16), grads)
            for half, g in enumerate((gkeys, gvalues)):
                columns = slice(half * cols, (half + 1) * cols)
                for n in range(3):
                    place = loc(k + n, j, BLK)
                    if k == 0 or n == 2:
                        acc[place, columns] = g[n * BLK : (n + 1) * BLK]
                    else:
                        acc[place, columns] += g[n * BLK : (n + 1) * BLK]
                spare[k * per_plane + j, :, columns] = g[fixed:]

    def collect(e):
        @pl.loop(0, per_plane)
        def _(t):
            at = pl.ds(pl.multiple_of(e * PLANE_TOK + t * BLK, BLK), BLK)
            value = acc[at, :]
            for k in range(max(e - 2, 0), min(e, last) + 1):
                for step in range(1, per_plane):
                    j = lax.rem(t + step, per_plane)
                    off = free_slot(k, j) - (e * per_plane + t)
                    hit = (1 - jnp.minimum(off * off, 1)).astype(F32)
                    value = value + hit * spare[k * per_plane + j]
            if 1 <= e <= planes:
                acc[at, :] = value
            low[at, :] = value.astype(BF16)

    returns = {}

    def give_back(side, e):
        rows = loc(e, 0, PLANE_TOK)
        returns[side] = launch(
            copy_to(
                low.at[rows], from_halo.at[side], h_send.at[side], h_recv.at[side], sides[side]
            )
        )

    mixes = {}

    def mix_heads(k):
        rows = nat(k, 0, PLANE_TOK)
        mix_out[rows, :] = mm(attn[rows, :], ow_ref[:, theirs]).astype(BF16)
        mixes[k] = launch(
            copy_to(mix_out.at[rows], mix_in.at[rows], m_send.at[k], m_recv.at[k], mate)
        )
        mix[rows, :] = mm(attn[rows, :], ow_ref[:, mine])

    halo_keys(1, planes + 1)
    for k in reversed(range(planes)):
        if k == 0:
            halo_keys(0, 0)
        attention_forward(k)
        if k > 0:
            mix_heads(k)
    for k in range(planes):
        output_gradient(k)
        attention_backward(k)
        if k == 0:
            collect(0)
            give_back(0, 0)
            mix_heads(0)

    orders = (groups[:1] + groups[2:] + groups[1:2], groups)
    sizes = []
    for order_of in orders:
        left = [span]
        for _, size in order_of:
            left.append(left[-1] >> size)
        sizes.append(left)
    lows = [jnp.int32(0), jnp.int32(span)]
    trail = [[], []]
    step_of = [0, 0]
    flight = [[], []]
    links = [0, 0]

    def rows_at(at, size):
        return pl.ds(pl.multiple_of(at, 16), size)

    def travel(t, src, dst, where):
        n = links[t]
        links[t] = n + 1
        flight[t].append(launch(copy_to(src, dst, w_send.at[t, n], w_recv.at[t, n], where)))

    def slot_of(t, k, flip):
        size = sizes[t][k + 1]
        return pl.ds(span - sizes[t][k] + (flip - 1) * size, size)

    def advance(t):
        k = step_of[t]
        if k > 2 * stages:
            return
        for copy in flight[t]:
            copy.wait_recv()
        flight[t] = []
        if k == 2 * stages:
            for n in range(4):
                at = pl.ds(t * span + n * (span // 4), span // 4)
                stores.append(
                    pltpu.make_async_copy(
                        final.at[at], final_out_ref.at[at], store_sem.at[3 + 4 * t + n]
                    )
                )
                stores[-1].start()
        if 1 <= k <= stages:
            at = rows_at(lows[t], sizes[t][k])
            value = wsum[at, :]
            for flip in range(1, 1 << orders[t][k - 1][1]):
                value = value + incoming[t, slot_of(t, k - 1, flip), :].astype(F32)
            if k < stages:
                wsum[at, :] = value
            else:
                final[at, :] = value.astype(BF16)
        if k < stages:
            group, size = orders[t][k], sizes[t][k + 1]
            for flip in range(1, 1 << group[1]):
                slots = slot_of(t, k, flip)
                give = lows[t] + digit_of(group, flip) * size
                outgoing[t, slots, :] = wsum[rows_at(give, size), :].astype(BF16)
                travel(t, outgoing.at[t, slots], incoming.at[t, slots], peer(group, flip))
            lows[t] = lows[t] + digit_of(group, 0) * size
            trail[t].append(lows[t])
        elif k < 2 * stages:
            j = 2 * stages - 1 - k
            at = rows_at(trail[t][j], sizes[t][j + 1])
            for where in peers(orders[t][j]):
                travel(t, final.at[at], final.at[at], where)
        step_of[t] = k + 1

    def weight_gradient(base, rows, g):
        for index, s_ref in ((tp, so), (1 - tp, st)):
            product = mm_tn(s_ref[rows, :], g)
            for half in range(halves):
                at = pl.multiple_of(base + half * depth + index * width, 128)
                wsum[pl.ds(at, width), :] = product[:, half * 128 : (half + 1) * 128]

    block = depth * halves
    inside = slice(PLANE_TOK, PLANE_TOK + tokens)
    weight_gradient(0, inside, gq_all[...])
    for index, c_ref in ((tp, cot_ref), (1 - tp, ct)):
        product = mm_tn(attn[...], c_ref[...])
        for half in range(width // 128):
            wsum[pl.ds(pl.multiple_of(block + (index * (width // 128) + half) * cols, 128), cols), :] = (
                product[:, half * 128 : (half + 1) * 128]
            )
    advance(0)
    collect(planes + 1)
    give_back(1, planes + 1)
    for e in range(1, planes + 1):
        collect(e)
    everything = slice(0, low.shape[0])
    weight_gradient(2 * block, everything, low[:, :cols])
    weight_gradient(3 * block, everything, low[:, cols:])
    advance(1)
    advance(0)
    for k in range(planes):
        for c in range(pieces):
            rows = loc(k, c)
            gq = gq_all[rows, :]
            own[rows, :] = mm_nt(gq, wq_ref[mine, :])
            other[rows, :] = mm_nt(gq, wq_ref[theirs, :])
    advance(1)
    parts = {}
    stores = []

    def mix_add():
        for k in reversed(range(planes)):
            rows = nat(k, 0, PLANE_TOK)
            mixes[k].wait_recv()
            layer_ref[rows, :] = (
                so[loc(k + 1, 0, PLANE_TOK), :].astype(F32)
                + (mix[rows, :] + mix_in[rows, :].astype(F32))
            ).astype(BF16)
        stores.append(pltpu.make_async_copy(layer_ref, layer_out_ref, store_sem.at[0]))
        stores[-1].start()

    for k in reversed(range(planes)):
        for side, _ in edges_of(k):
            returns[side].wait_recv()
        for c in range(pieces):
            rows = loc(k, c)
            value = acc[loc(k + 1, c), :]
            for side, _ in edges_of(k):
                value = value + from_halo[side, loc(0, c), :].astype(F32)
            value = value.astype(BF16)
            gk, gv = value[:, :cols], value[:, cols:]
            part_out[rows, :] = (
                other[rows, :] + mm_nt(gk, wk_ref[theirs, :]) + mm_nt(gv, wv_ref[theirs, :])
            ).astype(BF16)
            parts[k, c] = launch(
                copy_to(
                    part_out.at[rows], part_in.at[rows],
                    p_send.at[k * pieces + c], p_recv.at[k * pieces + c], mate,
                )
            )
            own[rows, :] += mm_nt(gk, wk_ref[mine, :]) + mm_nt(gv, wv_ref[mine, :])
        if k == last:
            mix_add()
    advance(1)
    edges = {}
    sums = [jnp.zeros((1, width), F32) for _ in range(3)]
    turns = [(), (0,), (0, 1), ()]
    for k in reversed(range(planes)):
        for c in range(pieces):
            rows = loc(k, c)
            parts[k, c].wait_recv()
            stem_grad = cot_ref[nat(k, c), :].astype(F32) + (
                own[rows, :] + part_in[rows, :].astype(F32)
            )
            own[rows, :] = stem_grad
            for side, _ in edges_of(k):
                at = loc(side, c)
                edge[at, :] = stem_grad.astype(BF16)
                edges[side, c] = launch(
                    copy_to(
                        edge.at[at], edge_in.at[at],
                        e_send.at[side, c], e_recv.at[side, c], sides[side],
                    )
                )
            for n in range(3):
                sums[n] = sums[n] + jnp.sum(
                    stem_grad * tokens_at(k - 1 + n, c), axis=0, keepdims=True
                )
            for t in turns.pop(0) if turns else ():
                advance(t)
    swap = core == 1
    sums = [jnp.where(swap, sums[2], sums[0]), sums[1], jnp.where(swap, sums[0], sums[2])]
    taps_sum[0] = jnp.concatenate(sums + [jnp.zeros((5, width), F32)], axis=0)

    def send_taps(k):
        base = sum((1 << size) - 1 for _, size in tap_groups[:k])
        return [
            launch(
                copy_to(
                    taps_sum.at[k], taps_in.at[base + n],
                    g_send.at[base + n], g_recv.at[base + n], where,
                )
            )
            for n, where in enumerate(peers(tap_groups[k]))
        ]

    def take_taps(k, copies):
        base = sum((1 << size) - 1 for _, size in tap_groups[:k])
        value = taps_sum[k]
        for n, copy in enumerate(copies):
            copy.wait_recv()
            value = value + taps_in[base + n]
        taps_sum[k + 1] = value

    def gradient_at(k, c):
        if k < 0:
            return edge_in[loc(0, c), :].astype(F32)
        if k > last:
            return edge_in[loc(1, c), :].astype(F32)
        return own[loc(k, c), :]

    def finish_tokens():
        for copy in edges.values():
            copy.wait_recv()
        for k in range(planes):
            for c in range(pieces):
                grad_ref[nat(k, c), :] = (
                    tap_low * gradient_at(k + 1, c) + tap_mid * gradient_at(k, c)
                    + tap_high * gradient_at(k - 1, c)
                )
        stores.append(pltpu.make_async_copy(grad_ref, grad_out_ref, store_sem.at[1]))
        stores[-1].start()

    for k in range(len(tap_groups)):
        copies = send_taps(k)
        advance(0)
        advance(1)
        if k == 0:
            finish_tokens()
        take_taps(k, copies)
    for _ in range(2 * stages):
        advance(0)
        advance(1)
    stores.append(
        pltpu.make_async_copy(taps_sum.at[len(tap_groups)], taps_out_ref, store_sem.at[2])
    )
    stores[-1].start()
    for store in stores:
        store.wait()
    for copy in sent:
        copy.wait_send()


def unpack_kernel(
    final_in, taps_in, layer_in, grad_in, gqw_ref, gkw_ref, gvw_ref, go_ref, taps_ref,
    layer_ref, grad_ref, final, taps, layer, grad, gqw, gkw, gvw, go, load_sem, sem,
):
    loads, stores = [], []

    def move(kept, semaphores, src, dst):
        kept.append(pltpu.make_async_copy(src, dst, semaphores.at[len(kept)]))
        kept[-1].start()

    def cut(ref, count):
        rows = ref.shape[0] // count
        return [pl.ds(n * rows, rows) for n in range(count)]

    outs = ((gqw, gqw_ref), (go, go_ref), (gkw, gkw_ref), (gvw, gvw_ref))
    at = 0
    for out, _ in outs:
        for _ in range(out.shape[1] // 128):
            piece = pl.ds(at, out.shape[0])
            move(loads, load_sem, final_in.at[piece], final.at[piece])
            at += out.shape[0]
    first = len(loads)
    passing = [(taps_in, taps, taps_ref, None)]
    passing += [(layer_in, layer, layer_ref, piece) for piece in cut(layer, 2)]
    passing += [(grad_in, grad, grad_ref, piece) for piece in cut(grad, 4)]
    for src, here, _, piece in passing:
        if piece is None:
            move(loads, load_sem, src, here)
        else:
            move(loads, load_sem, src.at[piece], here.at[piece])
    at = turn = 0
    for out, dst in outs:
        for half in range(out.shape[1] // 128):
            loads[turn].wait()
            out[:, half * 128 : (half + 1) * 128] = final[at : at + out.shape[0], :].astype(F32)
            at += out.shape[0]
            turn += 1
        for piece in cut(out, 2):
            move(stores, sem, out.at[piece], dst.at[piece])
    for n, (_, here, dst, piece) in enumerate(passing):
        loads[first + n].wait()
        if piece is None:
            move(stores, sem, here.at[0 : dst.shape[0]], dst)
        else:
            move(stores, sem, here.at[piece], dst.at[piece])
    for store in stores:
        store.wait()


def body(
    slabs,
    tokens,
    stem_taps,
    query_weight,
    key_weight,
    value_weight,
    out_weight,
    key_blocks,
    counts,
    cotangent,
):
    count, width = tokens.shape
    depth, cols = query_weight.shape
    plane = PLANE_TOK
    planes = count // plane
    sds = jax.ShapeDtypeStruct
    count_bits = slabs.bit_length() - 1
    radix = [2, 2] + [1 << min(2, count_bits - b) for b in range(2, count_bits, 2)]
    links = sum(radix) - len(radix)
    tap_radix = [2] + [1 << min(3, count_bits - b) for b in range(1, count_bits, 3)]
    tap_links = sum(tap_radix) - len(tap_radix)
    chunks = count // CHUNK
    pieces = plane // CHUNK
    blocks = count // BLK
    wide = count + 2 * plane
    dma = pltpu.SemaphoreType.DMA
    rows = 4 * depth * cols // 128
    semaphores = [
        (2, pieces),
        (chunks,),
        (chunks,),
        (2, pieces),
        (2, pieces),
        (2,),
        (planes,),
        (chunks,),
        (2, pieces),
        (2, 2 * links),
        (tap_links,),
    ]
    layer_out, grad_tokens, final, taps = pl.pallas_call(
        functools.partial(layer_kernel, slabs),
        out_shape=[
            sds((count, width), BF16),
            sds((count, width), F32),
            sds((rows, 128), BF16),
            sds((8, width), F32),
        ],
        in_specs=[HBM] * 9,
        out_specs=[HBM] * 4,
        scratch_shapes=[
            pltpu.SMEM((MAXK, blocks), jnp.int32),
            pltpu.SMEM((blocks,), jnp.int32),
            pltpu.VMEM((count, width), BF16),
            pltpu.VMEM((count, width), BF16),
            pltpu.VMEM(stem_taps.shape, F32),
            pltpu.VMEM((depth, cols), BF16),
            pltpu.VMEM((depth, cols), BF16),
            pltpu.VMEM((depth, cols), BF16),
            pltpu.VMEM((cols, depth), BF16),
            pltpu.VMEM((count, width), BF16),
            pltpu.VMEM((count, width), F32),
            pltpu.VMEM((rows, 128), BF16),
            dma((9,)),
            dma((11,)),
            pltpu.VMEM((2, plane, width), BF16),
            pltpu.VMEM((wide, width), BF16),
            pltpu.VMEM((wide, width), BF16),
            pltpu.VMEM((count, width), BF16),
            pltpu.VMEM((count, cols), BF16),
            pltpu.VMEM((wide // BLK, BLK, 2 * cols), BF16),
            pltpu.VMEM((count, cols), BF16),
            pltpu.VMEM((count, cols), BF16),
            pltpu.VMEM((wide, 2 * cols), F32),
            pltpu.VMEM((blocks, BLK, 2 * cols), F32),
            pltpu.VMEM((blocks, MAXK * BLK, cols // HD * BLK), F32),
            pltpu.VMEM((count, cols), BF16),
            pltpu.VMEM((wide, 2 * cols), BF16),
            pltpu.VMEM((2, plane, 2 * cols), BF16),
            pltpu.VMEM((count, width), F32),
            pltpu.VMEM((count, width), BF16),
            pltpu.VMEM((count, width), BF16),
            pltpu.VMEM((count, width), F32),
            pltpu.VMEM((count, width), F32),
            pltpu.VMEM((count, width), BF16),
            pltpu.VMEM((count, width), BF16),
            pltpu.VMEM((2 * plane, width), BF16),
            pltpu.VMEM((2 * plane, width), BF16),
            pltpu.VMEM((rows, 128), F32),
            pltpu.VMEM((2, rows // 2, 128), BF16),
            pltpu.VMEM((2, rows // 2, 128), BF16),
            pltpu.VMEM((tap_links, 8, width), F32),
            pltpu.VMEM((len(tap_radix) + 1, 8, width), F32),
        ]
        + [dma(shape) for shape in semaphores for _ in range(2)],
        compiler_params=pltpu.CompilerParams(
            collective_id=0, has_side_effects=True, vmem_limit_bytes=60 * MIB
        ),
    )(
        key_blocks.T,
        counts,
        tokens,
        cotangent,
        stem_taps,
        query_weight,
        key_weight,
        value_weight,
        out_weight,
    )
    weight = sds((depth, cols), F32)
    out_grad = sds((cols, depth), F32)
    gqw, gkw, gvw, go, grad_taps, layer_out, grad_tokens = pl.pallas_call(
        unpack_kernel,
        out_shape=[
            weight,
            weight,
            weight,
            out_grad,
            sds(stem_taps.shape, F32),
            sds((count, width), BF16),
            sds((count, width), F32),
        ],
        in_specs=[HBM] * 4,
        out_specs=[HBM] * 7,
        scratch_shapes=[
            pltpu.VMEM(x.shape, x.dtype)
            for x in (final, taps, layer_out, grad_tokens, weight, weight, weight, out_grad)
        ]
        + [dma((rows // 256 + 7,)), dma((15,))],
        compiler_params=pltpu.CompilerParams(vmem_limit_bytes=60 * MIB),
    )(final, taps, layer_out, grad_tokens)
    return (layer_out, grad_tokens, grad_taps, gqw, gkw, gvw, go)


def solution(mesh):
    in_specs = (
        P("slab", "tp"),
        P(None, "tp"),
        P(None, "tp"),
        P(None, "tp"),
        P(None, "tp"),
        P("tp", None),
        P("slab", None),
        P("slab"),
        P("slab", "tp"),
    )
    out_specs = (
        P("slab", "tp"),
        P("slab", "tp"),
        P(None, "tp"),
        P(None, "tp"),
        P(None, "tp"),
        P(None, "tp"),
        P("tp", None),
    )
    return jax.shard_map(
        functools.partial(body, mesh.shape["slab"]),
        mesh=mesh,
        in_specs=in_specs,
        out_specs=out_specs,
        check_vma=False,
    )
```
